1024 devices in a mesh: seq: 16 (over y_hi, x, core), zero: 64 (over z, y_lo).
Axes of the slice: x: 4, y: 8 (y_hi: 2, y_lo: 4; y = y_hi * 4 + y_lo), z: 16, core: 2. Of those that a mesh axis runs over, the one named last changes fastest.
Arguments:
- inputs: bfloat16 [64, 4096, 1024], P('zero', 'seq'), may hold values from -16 to 16
- queries: bfloat16 [64, 4096, 512], P('zero', 'seq'), may hold values from -6 to 6
- values: bfloat16 [64, 4096, 512], P('zero', 'seq'), may hold values from -6 to 6
- w_key: bfloat16 [1024, 512], P('zero'), may hold values from -0.1875 to 0.1875
- state_in: float32 [64, 4, 128, 128], P('zero'), may hold values from -96 to 96
- norm_in: float32 [64, 4, 128], P('zero'), may hold values from 0.125 to 2048
- out_gain: float32 [512], replicated, may hold values from 0.5 to 1.5
- out_grad: bfloat16 [64, 4096, 512], P('zero', 'seq'), may hold values from -6 to 6
Outputs:
- attended: bfloat16 [64, 4096, 512], P('zero', 'seq')
- inputs_grad: bfloat16 [64, 4096, 1024], P('zero', 'seq')
- queries_grad: bfloat16 [64, 4096, 512], P('zero', 'seq')
- values_grad: bfloat16 [64, 4096, 512], P('zero', 'seq')
- w_key_grad: float32 [1024, 512], P(('seq', 'zero'))
The draws below stay inside these ranges and needn't reach their ends.
All inputs are finite; a program needn't handle non-finite values.
Results may differ from the reference program's by a relative error of at most 0.015.
Values may be sent and summed in bfloat16 or wider, within the bound.
A program may use at most 64 MiB of HBM per device.

```python
import math
import jax
import jax.numpy as jnp
from jax import lax

D = 1024
H = 4
DH = 128
TOK_DEV = 256
HD = 512
LEN = 4096
DOCS = 64


def raised(drawn, key, source, target, shards_of, factor):
    def block_of(axis_at):
        return (jnp.arange(drawn.shape[axis_at]) // (drawn.shape[axis_at] // shards_of)).reshape((-1,) + (1,) * (drawn.ndim - 1 - axis_at))

    one_side = jax.random.permutation(key, shards_of)[block_of(target)]
    far = (block_of(target) + shards_of // 2) % shards_of
    return jnp.where((block_of(source) == one_side) | (block_of(source) == far), factor * drawn, drawn)


def block_levels(key, shape, cuts, smallest, high):
    def one(position, parts):
        steps = jax.random.uniform(jax.random.fold_in(jax.random.fold_in(key, 6), position), (parts,), jnp.float32, smallest / len(cuts), high / len(cuts))
        return jnp.repeat(jnp.exp(steps), shape[position] // parts).reshape((-1,) + (1,) * (len(shape) - position - 1))

    factor_of = one(*cuts[0])
    for cut in cuts[1:]:
        factor_of = factor_of * one(*cut)
    return factor_of


def bell_draw(own_key, dims, scale, bound, split=(), held_as=jnp.bfloat16):
    factor_of = block_levels(own_key, dims, split, -0.22, 0.18) if split else 1.0
    array = jax.random.normal(own_key, dims, jnp.float32) * scale * factor_of
    return jnp.minimum(jnp.maximum(array, -bound), bound).astype(held_as)


def bell_draw_with(key, shape, width, bound, pieces, heavy, dtype=jnp.bfloat16):
    values = width * jax.random.normal(key, shape, jnp.float32)
    if pieces:
        values = values * block_levels(key, shape, pieces, -0.22, 0.18)
    return jnp.clip(raised(values, jax.random.fold_in(key, 3), *heavy), -bound, bound).astype(dtype)


def setup_inputs(seed: int = 0) -> dict:
    arg_keys = jax.random.split(jax.random.key(seed), 9)
    inputs = bell_draw_with(arg_keys[0], (DOCS, LEN, D), 1.0, 16.0, ((0, 64), (1, 16)), (0, 2, 64, 4.0))
    queries = bell_draw(arg_keys[1], (DOCS, LEN, HD), 1.0, 6.0, ((0, 64), (1, 16)))
    values = bell_draw(arg_keys[2], (DOCS, LEN, HD), 1.0, 6.0, ((0, 64), (1, 16)))
    w_key = bell_draw(arg_keys[3], (D, HD), D ** -0.5, 0.1875, ((0, 64),))
    state_in = bell_draw(arg_keys[4], (DOCS, H, DH, DH), (TOK_DEV ** 0.5), 96.0, ((0, 64),), jnp.float32)
    norm_in = jnp.clip(jnp.exp(math.log(2048.0) - 9.704061 * jax.random.uniform(arg_keys[5], (DOCS, H, DH), jnp.float32) ** block_levels(arg_keys[5], (DOCS, H, DH), ((0, 64),), -0.2, 0.2)), 0.125, 2048.0)
    out_gain = jnp.clip(1.0 + 0.1 * jax.random.normal(arg_keys[6], (HD,), jnp.float32), 0.5, 1.5)
    out_grad = bell_draw(arg_keys[7], (DOCS, LEN, HD), 1.0, 6.0, ((0, 64), (1, 16)))
    return dict(inputs=inputs, queries=queries, values=values, w_key=w_key, state_in=state_in, norm_in=norm_in, out_gain=out_gain, out_grad=out_grad)


highest = lax.Precision.HIGHEST
epsilon = 1e-06

def feature(inner_values):
    return jax.nn.elu(inner_values) + 1.0

def slope(inner_values):
    return jnp.where(inner_values > 0, 1.0, jnp.exp(jnp.minimum(inner_values, 0.0)))

def round_back(inner_values):
    return lax.optimization_barrier(inner_values.astype(jnp.bfloat16)).astype(jnp.float32)

def one_document(inputs, queries, values, state_in, norm_in, out_grad, w_key, out_gain):
    blocks = LEN // TOK_DEV
    shape = (blocks, TOK_DEV, H, DH)
    key_lin = jnp.dot(inputs, w_key, preferred_element_type=jnp.float32)
    feat_key = feature(key_lin).astype(jnp.bfloat16)
    query_lin = queries.astype(jnp.float32)
    feat_query = feature(query_lin).astype(jnp.bfloat16)
    keys_f = feat_key.reshape(shape).astype(jnp.float32)
    query_f = feat_query.reshape(shape).astype(jnp.float32)
    values_f = values.reshape(shape).astype(jnp.float32)
    block_kv = jnp.einsum('cthd,cthe->chde', keys_f, values_f, precision=highest)
    block_z = lax.optimization_barrier(jnp.sum(keys_f, axis=1))
    cum_kv = jnp.cumsum(block_kv, axis=0)
    cum_z = jnp.cumsum(block_z, axis=0)
    state_now = state_in[None] + jnp.concatenate([jnp.zeros_like(block_kv[:1]), cum_kv[:-1]], axis=0)
    norm_now = norm_in[None] + jnp.concatenate([jnp.zeros_like(block_z[:1]), cum_z[:-1]], axis=0)
    causal = jnp.arange(TOK_DEV)[:, None] >= jnp.arange(TOK_DEV)[None, :]
    scores = jnp.einsum('cthd,cshd->chts', query_f, keys_f, precision=highest)
    weights = round_back(jnp.where(causal, scores, 0.0))
    numerator = jnp.einsum('chts,cshe->cthe', weights, values_f, precision=highest)
    numerator = numerator + jnp.einsum('cthd,chde->cthe', query_f, state_now, precision=highest)
    denominator = jnp.transpose(lax.optimization_barrier(jnp.sum(weights, axis=-1)), (0, 2, 1))
    denominator = denominator + jnp.einsum('cthd,chd->cth', query_f, norm_now, precision=highest)
    head_out = numerator / denominator[..., None]
    flat_out = head_out.reshape(blocks, TOK_DEV, HD)
    inv_rms = lax.rsqrt(lax.optimization_barrier(jnp.mean(flat_out * flat_out, axis=-1, keepdims=True)) + epsilon)
    attended = (flat_out * inv_rms * out_gain).astype(jnp.bfloat16)
    scaled = out_grad.reshape(blocks, TOK_DEV, HD).astype(jnp.float32) * out_gain
    inner = lax.optimization_barrier(jnp.mean(scaled * flat_out, axis=-1, keepdims=True))
    d_head = (inv_rms * (scaled - flat_out * inner * inv_rms * inv_rms)).reshape(shape)
    grad_num = round_back(d_head / denominator[..., None])
    grad_den = -lax.optimization_barrier(jnp.sum(d_head * head_out, axis=-1)) / denominator
    d_weights = jnp.einsum('cthe,cshe->chts', grad_num, values_f, precision=highest)
    d_weights = d_weights + jnp.transpose(grad_den, (0, 2, 1))[..., None]
    d_weights = round_back(jnp.where(causal, d_weights, 0.0))
    ds_local = jnp.einsum('cthd,cthe->chde', query_f, grad_num, precision=highest)
    dz_local = jnp.einsum('cth,cthd->chd', grad_den, query_f, precision=highest)
    back_s = jnp.flip(jnp.cumsum(jnp.flip(ds_local, 0), axis=0), 0)
    back_z = jnp.flip(jnp.cumsum(jnp.flip(dz_local, 0), axis=0), 0)
    carry_s = jnp.concatenate([back_s[1:], jnp.zeros_like(ds_local[:1])], axis=0)
    carry_z = jnp.concatenate([back_z[1:], jnp.zeros_like(dz_local[:1])], axis=0)
    d_feat_key = jnp.einsum('chts,cthd->cshd', d_weights, query_f, precision=highest)
    d_feat_key = d_feat_key + jnp.einsum('cshe,chde->cshd', values_f, carry_s, precision=highest)
    d_feat_key = d_feat_key + carry_z[:, None]
    d_value = jnp.einsum('chts,cthe->cshe', weights, grad_num, precision=highest)
    d_value = d_value + jnp.einsum('cshd,chde->cshe', keys_f, carry_s, precision=highest)
    d_feat_query = jnp.einsum('chts,cshd->cthd', d_weights, keys_f, precision=highest)
    d_feat_query = d_feat_query + jnp.einsum('cthe,chde->cthd', grad_num, state_now, precision=highest)
    d_feat_query = d_feat_query + grad_den[..., None] * norm_now[:, None]
    d_key = (d_feat_key.reshape(LEN, HD) * slope(key_lin)).astype(jnp.bfloat16)
    values_grad = d_value.reshape(LEN, HD).astype(jnp.bfloat16)
    queries_grad = (d_feat_query.reshape(LEN, HD) * slope(query_lin)).astype(jnp.bfloat16)
    inputs_grad = jnp.dot(d_key, w_key.T, preferred_element_type=jnp.float32).astype(jnp.bfloat16)
    key_grad = jnp.dot(inputs.T, d_key, preferred_element_type=jnp.float32)
    return (attended.reshape(LEN, HD), inputs_grad, queries_grad, values_grad, key_grad)

def reference(inputs, queries, values, w_key, state_in, norm_in, out_gain, out_grad):

    def visit(carry, items):
        result = one_document(items[0], items[1], items[2], items[3], items[4], items[5], w_key, out_gain)
        return (carry + result[4], (result[0], result[1], result[2], result[3]))
    start = jnp.zeros((D, HD), jnp.float32)
    totals, outputs = lax.scan(visit, start, (inputs, queries, values, state_in, norm_in, out_grad))
    return (outputs[0], outputs[1], outputs[2], outputs[3], totals)
```

```python
import jax
import jax.numpy as jnp
from jax import lax
from jax.experimental import pallas as pl
from jax.experimental.pallas import tpu as pltpu
from jax.sharding import PartitionSpec as P

epsilon = 1e-06
MESH = pl.DeviceIdType.MESH
F32 = jnp.float32
BF16 = jnp.bfloat16

Y_HI, X, CORES = 2, 4, 2
Z, Y_LO = 16, 4
GROUP = X * CORES
RING_Y = Y_HI * Y_LO
HEADS, HEAD = 4, 128
WIDTH = HEADS * HEAD


def dot(a, b):
    return jnp.dot(a, b, preferred_element_type=F32)


def dot_nt(a, b):
    return lax.dot_general(a, b, (((1,), (1,)), ((), ())), preferred_element_type=F32)


def dot_tn(a, b):
    return lax.dot_general(a, b, (((0,), (0,)), ((), ())), preferred_element_type=F32)


def wide(value):
    return value.astype(F32)


def features(value):
    low = jnp.exp(jnp.minimum(value, 0.0))
    positive = value > 0
    return jnp.where(positive, value + 1.0, low), jnp.where(positive, 1.0, low)


def body(
    inp, q, v, w, st, nm, gain, og,
    att, ig, qg, vg, wg,
    wf, inpt, fq, slq, fk, slk, wts, numi, deni, ho, rec, gn, gd, state, dfk, dval, dk, norm,
    f_out, f_in, f_tot, f_tot_in, f_pre, f_ret,
    b_out, b_in, b_tot, b_tot_in, b_pre, b_ret,
    gown, gsend, grecv, xsend, xrecv, ykeep, ysend, yrecv, zsend, zrecv,
    local_sem,
    wz_s, wz_r, wy_s, wy_r, wx_s, wx_r, wc_s, wc_r,
    fa_s, fa_r, fy_s, fy_r, fb_s, fb_r,
    ba_s, ba_r, by_s, by_r, bb_s, bb_r,
    rc_s, rc_r, rx_s, rx_r, ry_s, ry_r, rz_s, rz_r,
):
    seq, zero = lax.axis_index("seq"), lax.axis_index("zero")
    core = lax.rem(seq, CORES)
    x = lax.rem(seq // CORES, X)
    y_hi = seq // GROUP
    z = zero // Y_LO
    y_lo = lax.rem(zero, Y_LO)
    y = y_hi * Y_LO + y_lo
    own = x * CORES + core
    partner = seq + 1 - 2 * core
    tokens, model = inp.shape
    depth = w.shape[0]
    half = depth // CORES
    block = WIDTH // X

    def send(source, target, s_sem, r_sem, to_seq, to_zero):
        return pltpu.make_async_remote_copy(
            src_ref=source,
            dst_ref=target,
            send_sem=s_sem,
            recv_sem=r_sem,
            device_id={"seq": to_seq, "zero": to_zero},
            device_id_type=MESH,
        )

    def along_z(k):
        return seq, lax.rem(z + k, Z) * Y_LO + y_lo

    def along_y(k):
        there = lax.rem(y + k + RING_Y, RING_Y)
        return (
            (there // Y_LO) * GROUP + own,
            z * Y_LO + lax.rem(there, Y_LO),
        )

    def along_x(k):
        return y_hi * GROUP + lax.rem(x + k, X) * CORES + core, zero

    def in_group(k):
        return y_hi * GROUP + lax.rem(own + k, GROUP), zero

    barrier = pltpu.get_barrier_semaphore()

    def greet(place):
        pl.semaphore_signal(
            barrier, inc=1, device_id={"seq": place[0], "zero": place[1]}, device_id_type=MESH
        )

    def greet_z(k, carry):
        greet(along_z(k))
        return carry

    lax.fori_loop(1, Z, greet_z, 0)
    for k in range(1, RING_Y):
        greet(along_y(k))
    for k in range(1, GROUP):
        greet(in_group(k))
    pl.semaphore_wait(barrier, Z + RING_Y + GROUP - 3)

    sent = []

    def rows_of(c):
        return pl.ds(pl.multiple_of(c * half, half), half)

    def columns_of(xx):
        return pl.ds(pl.multiple_of(xx * block, block), block)

    rows, columns = rows_of(core), columns_of(x)

    def z_copy(k):
        return send(
            w.at[rows, columns], wf.at[z, y_lo, rows, columns],
            wz_s.at[k - 1], wz_r.at[k - 1], *along_z(k),
        )

    def z_arrival(k):
        origin = lax.rem(z - k + Z, Z)
        return send(
            w.at[rows, columns], wf.at[origin, y_lo, rows, columns],
            wz_s.at[k - 1], wz_r.at[k - 1], *along_z(k),
        )

    def far_first(n):
        return Z // 2 + ((n + 1) // 2) * (1 - 2 * lax.rem(n, 2))

    def z_start(n, carry):
        z_copy(far_first(n)).start()
        return carry

    lax.fori_loop(0, Z - 1, z_start, 0)
    keep = pltpu.make_async_copy(
        w.at[rows, columns], wf.at[z, y_lo, rows, columns], local_sem.at[0]
    )
    keep.start()

    span = CORES * Z * Y_LO
    j = lax.broadcasted_iota(jnp.int32, (span, span), 0)
    i = lax.broadcasted_iota(jnp.int32, (span, span), 1)
    within = lax.rem(j, Z * Y_LO)
    source = (j - within) + lax.rem(within, Z) * Y_LO + within // Z
    pick = jnp.where(source == i, 1.0, 0.0).astype(BF16)
    for b in range(Y_HI * X):
        turned = dot_nt(pick, inp[:, b * span : (b + 1) * span]).astype(BF16)
        for c in range(CORES):
            inpt[b // X, b % X, c] = turned[c * (span // CORES) : (c + 1) * (span // CORES)]
    for h in range(HEADS):
        lanes = slice(h * HEAD, (h + 1) * HEAD)
        feat, slope = features(wide(q[:, lanes]))
        fq[:, lanes] = feat.astype(BF16)
        slq[:, lanes] = slope

    def z_wait(k, carry):
        z_arrival(k).wait_recv()
        return carry

    keep.wait()
    lax.fori_loop(1, Z, z_wait, 0)

    steps_y = [1, -1, 2 - 4 * core] if Y_LO == 4 else [1]

    def piece(n, k, r):
        lo = y_lo if n == 0 else lax.rem(y_lo - steps_y[n - 1] + 2 * Y_LO, Y_LO)
        return wf.at[:, lo, r, columns_of(lax.rem(x - k + X, X))]

    def y_copy(n, at):
        return send(at, at, wy_s.at[n], wy_r.at[n], *along_y(steps_y[n]))

    def x_copy(n, k, at):
        slot = n * (X - 1) + k - 1
        return send(at, at, wx_s.at[slot], wx_r.at[slot], *along_x(k))

    def c_copy(n, k, at):
        slot = n * X + k
        return send(at, at, wc_s.at[slot], wc_r.at[slot], partner, zero)

    def pass_on(n):
        at = piece(n, 0, rows)
        for k in (2, 1, 3) if X == 4 else range(1, X):
            copy = x_copy(n, k, at)
            copy.start()
            sent.append(copy)
        copy = c_copy(n, 0, at)
        copy.start()
        sent.append(copy)

    for n in range(len(steps_y)):
        copy = y_copy(n, piece(0, 0, rows))
        copy.start()
        sent.append(copy)
    pass_on(0)
    for n in range(len(steps_y)):
        y_copy(n, piece(n + 1, 0, rows)).wait_recv()
        pass_on(n + 1)
    for n in range(Y_LO):
        for k in range(1, X):
            at = piece(n, k, rows)
            x_copy(n, k, at).wait_recv()
            copy = c_copy(n, k, at)
            copy.start()
            sent.append(copy)
    other_rows = rows_of(1 - core)
    for n in range(Y_LO):
        for k in range(X):
            c_copy(n, k, piece(n, k, other_rows)).wait_recv()

    for h in range(HEADS):
        lanes = slice(h * HEAD, (h + 1) * HEAD)
        weight = wf[:, :, :, lanes].reshape(model, HEAD)
        feat, slope = features(dot(inp[...], weight))
        fk[:, lanes] = feat.astype(BF16)
        slk[:, lanes] = slope

    part = WIDTH // GROUP
    padded = f_out.shape[1]

    def scan_start(mats, sums, out, inside, s_sem, r_sem):
        per = HEAD // part if part <= HEAD else 1
        for h in range(HEADS):
            for p in range(per):
                slot = h * per + p
                out[slot, 0:part] = mats[h][p * part : (p + 1) * part].astype(BF16)
                out[slot, part:padded] = jnp.broadcast_to(sums[h], (padded - part, HEAD)).astype(
                    BF16
                )
        for k in range(1, GROUP):
            copy = send(
                out.at[lax.rem(own + k, GROUP)], inside.at[own],
                s_sem.at[k - 1], r_sem.at[k - 1], *in_group(k),
            )
            copy.start()
            sent.append(copy)
        inside[pl.ds(own, 1)] = out[pl.ds(own, 1)]

    def group_wait(buffer, s_sem, r_sem):
        for k in range(1, GROUP):
            at = buffer.at[lax.rem(own - k + GROUP, GROUP)]
            send(at, at, s_sem.at[k - 1], r_sem.at[k - 1], *in_group(k)).wait_recv()

    def scan_total(out, inside, total, total_in, s_sem, r_sem, y_s, y_r):
        group_wait(inside, s_sem, r_sem)
        running = wide(inside[0])
        for p in range(1, GROUP):
            running = running + wide(inside[p])
        total[...] = running.astype(BF16)
        copy = send(total, total_in, y_s.at[0], y_r.at[0], *along_y(Y_LO))
        copy.start()
        sent.append(copy)
        return copy

    def scan_back(inside, total_in, copy, taken, order, pre, ret, s_sem, r_sem):
        copy.wait_recv()
        running = wide(total_in[...]) * taken.astype(F32)
        for p in order:
            pre[p] = running.astype(BF16)
            running = running + wide(inside[p])
        for k in range(1, GROUP):
            copy = send(
                pre.at[lax.rem(own + k, GROUP)], ret.at[own],
                s_sem.at[k - 1], r_sem.at[k - 1], *in_group(k),
            )
            copy.start()
            sent.append(copy)
        ret[pl.ds(own, 1)] = pre[pl.ds(own, 1)]

    def scan_result(ret, h):
        per = HEAD // part
        mats = [ret[h * per + p, 0:part] for p in range(per)]
        mat = mats[0] if per == 1 else jnp.concatenate(mats, axis=0)
        return mat, wide(ret[h * per, part : part + 16])[0:1]

    mats, sums = [], []
    for h in range(HEADS):
        lanes = slice(h * HEAD, (h + 1) * HEAD)
        mats.append(dot_tn(fk[:, lanes], v[:, lanes]))
        sums.append(jnp.sum(wide(fk[:, lanes]), axis=0, keepdims=True))
    scan_start(mats, sums, f_out, f_in, fa_s, fa_r)

    causal = lax.broadcasted_iota(jnp.int32, (tokens, tokens), 0) >= lax.broadcasted_iota(
        jnp.int32, (tokens, tokens), 1
    )

    def inside_block(h):
        lanes = slice(h * HEAD, (h + 1) * HEAD)
        scores = dot_nt(fq[:, lanes], fk[:, lanes])
        weights = jnp.where(causal, scores, 0.0).astype(BF16)
        wts[h] = weights
        extended = jnp.concatenate([v[:, lanes], jnp.ones((tokens, HEAD), BF16)], axis=1)
        both = dot(weights, extended)
        numi[:, lanes] = both[:, :HEAD]
        deni[:, lanes] = both[:, HEAD:]

    for h in range(HEADS // 2):
        inside_block(h)
    swap = scan_total(f_out, f_in, f_tot, f_tot_in, fa_s, fa_r, fy_s, fy_r)
    for h in range(HEADS // 2, HEADS):
        inside_block(h)
    scan_back(f_in, f_tot_in, swap, y_hi, range(GROUP), f_pre, f_ret, fb_s, fb_r)
    group_wait(f_ret, fb_s, fb_r)

    squares = jnp.zeros((tokens, HEAD), F32)
    crossed = jnp.zeros((tokens, HEAD), F32)
    for h in range(HEADS):
        lanes = slice(h * HEAD, (h + 1) * HEAD)
        prior, prior_sum = scan_result(f_ret, h)
        now = (st[h] + wide(prior)).astype(BF16)
        norm_now = nm[h : h + 1] + prior_sum
        state[h] = now
        norm[h] = norm_now
        query = fq[:, lanes]
        numerator = numi[:, lanes] + dot(query, now)
        denominator = deni[:, lanes] + jnp.sum(wide(query) * norm_now, axis=1, keepdims=True)
        inverse = 1.0 / denominator
        out = numerator * inverse
        ho[:, lanes] = out
        rec[:, lanes] = inverse
        squares = squares + out * out
        crossed = crossed + wide(og[:, lanes]) * gain[:, lanes] * out
    inv_rms = lax.rsqrt(jnp.sum(squares, axis=1, keepdims=True) / WIDTH + epsilon)
    inner = jnp.sum(crossed, axis=1, keepdims=True) / WIDTH
    factor = inner * inv_rms * inv_rms
    mats, sums = [], []
    for h in range(HEADS):
        lanes = slice(h * HEAD, (h + 1) * HEAD)
        out = ho[:, lanes]
        d_head = inv_rms * (wide(og[:, lanes]) * gain[:, lanes] - out * factor)
        numerator_grad = (d_head * rec[:, lanes]).astype(BF16)
        denominator_grad = -jnp.sum(d_head * out, axis=1, keepdims=True) * rec[:, lanes]
        gn[:, lanes] = numerator_grad
        gd[:, lanes] = denominator_grad
        mats.append(dot_tn(fq[:, lanes], numerator_grad))
        sums.append(jnp.sum(denominator_grad * wide(fq[:, lanes]), axis=0, keepdims=True))
    scan_start(mats, sums, b_out, b_in, ba_s, ba_r)

    def block_grads(h):
        lanes = slice(h * HEAD, (h + 1) * HEAD)
        grad = gn[:, lanes]
        row_grad = gd[:, lanes]
        d_weights = dot_nt(grad, v[:, lanes]) + jnp.concatenate(
            [row_grad] * (tokens // HEAD), axis=1
        )
        d_weights = jnp.where(causal, d_weights, 0.0).astype(BF16)
        dfk[:, lanes] = dot_tn(d_weights, fq[:, lanes])
        dval[:, lanes] = dot_tn(wts[h], grad)
        d_query = dot(d_weights, fk[:, lanes]) + dot_nt(grad, state[h]) + row_grad * norm[h]
        qg[:, lanes] = (d_query * slq[:, lanes]).astype(BF16)

    for h in range(HEADS // 2):
        block_grads(h)
    swap = scan_total(b_out, b_in, b_tot, b_tot_in, ba_s, ba_r, by_s, by_r)
    for h in range(HEADS // 2, HEADS):
        block_grads(h)
    scan_back(
        b_in, b_tot_in, swap, 1 - y_hi, range(GROUP - 1, -1, -1), b_pre, b_ret, bb_s, bb_r
    )
    for h in range(HEADS):
        lanes = slice(h * HEAD, (h + 1) * HEAD)
        att[:, lanes] = (ho[:, lanes] * inv_rms * gain[:, lanes]).astype(BF16)
    group_wait(b_ret, bb_s, bb_r)
    for h in range(HEADS):
        lanes = slice(h * HEAD, (h + 1) * HEAD)
        carry, carry_sum = scan_result(b_ret, h)
        total = dfk[:, lanes] + dot_nt(v[:, lanes], carry) + carry_sum
        dk[:, lanes] = (total * slk[:, lanes]).astype(BF16)

    def partial_of(xx, c):
        left = jnp.concatenate([inpt[hi, xx, c] for hi in range(Y_HI)], axis=0)
        return dot(left, dk[...])

    order = (2, 1, 3, 0) if X == 4 else tuple(range(1, X)) + (0,)

    def rc_copy(k):
        return send(gsend.at[k], grecv.at[k], rc_s.at[k], rc_r.at[k], partner, zero)

    for k in order:
        gsend[k] = partial_of(lax.rem(x + k, X), 1 - core).astype(BF16)
        copy = rc_copy(k)
        copy.start()
        sent.append(copy)
    for k in order:
        gown[k] = partial_of(lax.rem(x + k, X), core)

    def rx_copy(k):
        return send(
            xsend.at[k - 1], xrecv.at[k - 1], rx_s.at[k - 1], rx_r.at[k - 1], *along_x(k)
        )

    for k in order:
        rc_copy(k).wait_recv()
        if k:
            xsend[k - 1] = (gown[k] + wide(grecv[k])).astype(BF16)
            copy = rx_copy(k)
            copy.start()
            sent.append(copy)

    for h in range(HEADS):
        lanes = slice(h * HEAD, (h + 1) * HEAD)
        carry, _ = scan_result(b_ret, h)
        vg[:, lanes] = (dval[:, lanes] + dot(fk[:, lanes], carry)).astype(BF16)
    ig[...] = dot_nt(dk[...], wf[...].reshape(model, WIDTH)).astype(BF16)

    for k in range(1, X):
        rx_copy(k).wait_recv()
    total = gown[0] + wide(grecv[0])
    for k in range(1, X):
        total = total + wide(xrecv[k - 1])
    for there in range(RING_Y):
        part_y = total[there * Z : (there + 1) * Z]
        ykeep[there] = part_y
        ysend[there] = part_y.astype(BF16)

    def ry_copy(k):
        return send(
            ysend.at[lax.rem(y + k, RING_Y)], yrecv.at[k - 1],
            ry_s.at[k - 1], ry_r.at[k - 1], *along_y(k),
        )

    for k in (4, 3, 5, 2, 6, 1, 7) if RING_Y == 8 else range(1, RING_Y):
        copy = ry_copy(k)
        copy.start()
        sent.append(copy)
    total = ykeep[pl.ds(y, 1)][0]
    for k in range(1, RING_Y):
        ry_copy(k).wait_recv()
        total = total + wide(yrecv[k - 1])
    zsend[:, 0, :] = total

    def rz_copy(k):
        return send(
            zsend.at[lax.rem(z + k, Z)], zrecv.at[k - 1],
            rz_s.at[k - 1], rz_r.at[k - 1], *along_z(k),
        )

    def rz_start(n, carry):
        rz_copy(far_first(n)).start()
        return carry

    lax.fori_loop(0, Z - 1, rz_start, 0)
    last = zsend[pl.ds(z, 1)][0]
    for k in range(1, Z):
        rz_copy(k).wait_recv()
        last = last + zrecv[k - 1]
    wg[...] = last

    for copy in sent:
        copy.wait_send()

    def z_sent(k, carry):
        z_copy(k).wait_send()
        rz_copy(k).wait_send()
        return carry

    lax.fori_loop(1, Z, z_sent, 0)


def shards(inputs, queries, values, w_key, state_in, norm_in, out_gain, out_grad):
    docs, tokens, model = inputs.shape
    depth = w_key.shape[0]
    part = WIDTH // GROUP
    padded = part + 16
    rows_out = Z * Y_LO
    dma = pltpu.SemaphoreType.DMA
    vmem = pltpu.VMEM
    scan_buffers = [
        vmem((GROUP, padded, HEAD), BF16),
        vmem((GROUP, padded, HEAD), BF16),
        vmem((padded, HEAD), BF16),
        vmem((padded, HEAD), BF16),
        vmem((GROUP, padded, HEAD), BF16),
        vmem((GROUP, padded, HEAD), BF16),
    ]
    scan_sems = [dma((GROUP - 1,))] * 2 + [dma((1,))] * 2 + [dma((GROUP - 1,))] * 2
    scratch = (
        [
            vmem((Z, Y_LO, depth, WIDTH), BF16),
            vmem((Y_HI, X, CORES, rows_out, tokens), BF16),
            vmem((tokens, WIDTH), BF16),
            vmem((tokens, WIDTH), F32),
            vmem((tokens, WIDTH), BF16),
            vmem((tokens, WIDTH), F32),
            vmem((HEADS, tokens, tokens), BF16),
            vmem((tokens, WIDTH), F32),
            vmem((tokens, WIDTH), F32),
            vmem((tokens, WIDTH), F32),
            vmem((tokens, WIDTH), F32),
            vmem((tokens, WIDTH), BF16),
            vmem((tokens, WIDTH), F32),
            vmem((HEADS, HEAD, HEAD), BF16),
            vmem((tokens, WIDTH), F32),
            vmem((tokens, WIDTH), F32),
            vmem((tokens, WIDTH), BF16),
            vmem((HEADS, 1, HEAD), F32),
        ]
        + scan_buffers
        + scan_buffers
        + [
            vmem((X, Y_HI * rows_out, WIDTH), F32),
            vmem((X, Y_HI * rows_out, WIDTH), BF16),
            vmem((X, Y_HI * rows_out, WIDTH), BF16),
            vmem((X - 1, Y_HI * rows_out, WIDTH), BF16),
            vmem((X - 1, Y_HI * rows_out, WIDTH), BF16),
            vmem((RING_Y, Z, WIDTH), F32),
            vmem((RING_Y, Z, WIDTH), BF16),
            vmem((RING_Y - 1, Z, WIDTH), BF16),
            vmem((Z, 1, WIDTH), F32),
            vmem((Z - 1, 1, WIDTH), F32),
        ]
        + [dma((1,))]
        + [dma((Z - 1,))] * 2
        + [dma((Y_LO - 1,))] * 2
        + [dma((Y_LO * (X - 1),))] * 2
        + [dma((Y_LO * X,))] * 2
        + scan_sems
        + scan_sems
        + [dma((X,))] * 2
        + [dma((X - 1,))] * 2
        + [dma((RING_Y - 1,))] * 2
        + [dma((Z - 1,))] * 2
    )
    space = pl.BlockSpec(memory_space=pltpu.VMEM)
    shape = jax.ShapeDtypeStruct
    outs = pl.pallas_call(
        body,
        out_shape=(
            shape((tokens, WIDTH), BF16),
            shape((tokens, model), BF16),
            shape((tokens, WIDTH), BF16),
            shape((tokens, WIDTH), BF16),
            shape((1, WIDTH), F32),
        ),
        in_specs=[space] * 8,
        out_specs=(space,) * 5,
        scratch_shapes=scratch,
        compiler_params=pltpu.CompilerParams(
            collective_id=0, has_side_effects=True, vmem_limit_bytes=56 * 1024 * 1024
        ),
    )(
        inputs[0],
        queries[0],
        values[0],
        w_key,
        state_in[0],
        norm_in[0],
        out_gain[None],
        out_grad[0],
    )
    return (outs[0][None], outs[1][None], outs[2][None], outs[3][None], outs[4])


def solution(mesh):
    return jax.shard_map(
        shards,
        mesh=mesh,
        in_specs=(
            P("zero", "seq", None),
            P("zero", "seq", None),
            P("zero", "seq", None),
            P("zero", None),
            P("zero", None, None, None),
            P("zero", None, None),
            P(),
            P("zero", "seq", None),
        ),
        out_specs=(
            P("zero", "seq", None),
            P("zero", "seq", None),
            P("zero", "seq", None),
            P("zero", "seq", None),
            P(("seq", "zero"), None),
        ),
        check_vma=False,
    )
```

```python
import jax
import jax.numpy as jnp
from jax import lax
from jax.experimental import pallas as pl
from jax.experimental.pallas import tpu as pltpu
from jax.sharding import PartitionSpec as P

epsilon = 1e-06
MESH = pl.DeviceIdType.MESH
F32 = jnp.float32
BF16 = jnp.bfloat16

Y_HI, X, CORES = 2, 4, 2
Z, Y_LO = 16, 4
GROUP = X * CORES
RING_Y = Y_HI * Y_LO
HEADS, HEAD = 4, 128
WIDTH = HEADS * HEAD


def dot(a, b):
    return jnp.dot(a, b, preferred_element_type=F32)


def dot_nt(a, b):
    return lax.dot_general(a, b, (((1,), (1,)), ((), ())), preferred_element_type=F32)


def dot_tn(a, b):
    return lax.dot_general(a, b, (((0,), (0,)), ((), ())), preferred_element_type=F32)


def wide(value):
    return value.astype(F32)


def features(value):
    low = jnp.exp(jnp.minimum(value, 0.0))
    positive = value > 0
    return jnp.where(positive, value + 1.0, low), jnp.where(positive, 1.0, low)


def body(
    inp_hbm, q_hbm, v_hbm, w, st_hbm, nm_hbm, gain_hbm, og_hbm,
    att, ig, qg, vg, wg,
    inp, q, v, st, nm, gain, og,
    wf, inpt, fq, slq, fk, slk, wts, numi, deni, ho, rec, gn, gd, state, dfk, dval, dk, norm,
    f_out, f_in, f_tot, f_tot_in, f_pre, f_ret,
    b_out, b_in, b_tot, b_tot_in, b_pre, b_ret,
    gown, gsend, grecv, vsend, vrecv, xsend, xrecv, ykeep, ysend, yrecv, zsend, zrecv,
    local_sem, load_sem,
    wz_s, wz_r, wy_s, wy_r, wx_s, wx_r, wc_s, wc_r,
    fa_s, fa_r, fy_s, fy_r, fb_s, fb_r,
    ba_s, ba_r, by_s, by_r, bb_s, bb_r,
    rc_s, rc_r, rv_s, rv_r, rx_s, rx_r, ry_s, ry_r, rz_s, rz_r,
):
    seq, zero = lax.axis_index("seq"), lax.axis_index("zero")
    core = lax.rem(seq, CORES)
    x = lax.rem(seq // CORES, X)
    y_hi = seq // GROUP
    z = zero // Y_LO
    y_lo = lax.rem(zero, Y_LO)
    y = y_hi * Y_LO + y_lo
    own = x * CORES + core
    partner = seq + 1 - 2 * core
    tokens, model = inp.shape
    depth = w.shape[0]
    half = depth // CORES
    wide_block = WIDTH // 2
    block = wide_block // 2
    side = lax.rem(x, 2)

    def send(source, target, s_sem, r_sem, to_seq, to_zero):
        return pltpu.make_async_remote_copy(
            src_ref=source,
            dst_ref=target,
            send_sem=s_sem,
            recv_sem=r_sem,
            device_id={"seq": to_seq, "zero": to_zero},
            device_id_type=MESH,
        )

    def along_z(k):
        return seq, lax.rem(z + k, Z) * Y_LO + y_lo

    def along_y(k):
        there = lax.rem(y + k + RING_Y, RING_Y)
        return (
            (there // Y_LO) * GROUP + own,
            z * Y_LO + lax.rem(there, Y_LO),
        )

    def along_x(k):
        return y_hi * GROUP + lax.rem(x + k, X) * CORES + core, zero

    def in_group(k):
        return y_hi * GROUP + lax.rem(own + k, GROUP), zero

    barrier = pltpu.get_barrier_semaphore()

    def greet(place):
        pl.semaphore_signal(
            barrier, inc=1, device_id={"seq": place[0], "zero": place[1]}, device_id_type=MESH
        )

    def greet_z(k, carry):
        greet(along_z(k))
        return carry

    lax.fori_loop(1, Z, greet_z, 0)
    for k in range(1, RING_Y):
        greet(along_y(k))
    for k in range(1, GROUP):
        greet(in_group(k))
    loads = [
        pltpu.make_async_copy(outer, inner, load_sem.at[n])
        for n, (outer, inner) in enumerate(
            (
                (inp_hbm, inp), (q_hbm, q), (v_hbm, v), (st_hbm, st),
                (nm_hbm, nm), (gain_hbm, gain), (og_hbm, og),
            )
        )
    ]
    for load in loads:
        load.start()
    pl.semaphore_wait(barrier, Z + RING_Y + GROUP - 3)

    sent = []

    def rows_of(c):
        return pl.ds(pl.multiple_of(c * half, half), half)

    def columns_of(which, quarter):
        return pl.ds(pl.multiple_of(which * wide_block + quarter * block, block), block)

    rows = rows_of(core)
    columns = pl.ds(pl.multiple_of(side * wide_block, wide_block), wide_block)

    def z_copy(k):
        return send(
            w.at[rows, columns], wf.at[z, y_lo, rows, columns],
            wz_s.at[k - 1], wz_r.at[k - 1], *along_z(k),
        )

    def z_arrival(k):
        origin = lax.rem(z - k + Z, Z)
        return send(
            w.at[rows, columns], wf.at[origin, y_lo, rows, columns],
            wz_s.at[k - 1], wz_r.at[k - 1], *along_z(k),
        )

    def far_first(n):
        return Z // 2 + ((n + 1) // 2) * (1 - 2 * lax.rem(n, 2))

    def z_start(n, carry):
        z_copy(far_first(n)).start()
        return carry

    lax.fori_loop(0, Z - 1, z_start, 0)
    keep = pltpu.make_async_copy(
        w.at[rows, columns], wf.at[z, y_lo, rows, columns], local_sem.at[0]
    )
    keep.start()

    for load in loads:
        load.wait()

    span = CORES * Z * Y_LO
    j = lax.broadcasted_iota(jnp.int32, (span, span), 0)
    i = lax.broadcasted_iota(jnp.int32, (span, span), 1)
    within = lax.rem(j, Z * Y_LO)
    source = (j - within) + lax.rem(within, Z) * Y_LO + within // Z
    pick = jnp.where(source == i, 1.0, 0.0).astype(BF16)
    for b in range(Y_HI * X):
        turned = dot_nt(pick, inp[:, b * span : (b + 1) * span]).astype(BF16)
        for c in range(CORES):
            inpt[b // X, b % X, c] = turned[c * (span // CORES) : (c + 1) * (span // CORES)]
    for h in range(HEADS):
        lanes = slice(h * HEAD, (h + 1) * HEAD)
        feat, slope = features(wide(q[:, lanes]))
        fq[:, lanes] = feat.astype(BF16)
        slq[:, lanes] = slope

    def z_wait(k, carry):
        z_arrival(k).wait_recv()
        return carry

    keep.wait()
    lax.fori_loop(1, Z, z_wait, 0)

    steps_y = [1, -1, 2 - 4 * core] if Y_LO == 4 else [1]

    def source_of(n):
        return y_lo if n == 0 else lax.rem(y_lo - steps_y[n - 1] + 2 * Y_LO, Y_LO)

    def y_copy(n, at):
        return send(at, at, wy_s.at[n], wy_r.at[n], *along_y(steps_y[n]))

    def x_copy(n, quarter, at):
        slot = n * 2 + quarter
        step = 1 if quarter == 0 else X - 1
        return send(at, at, wx_s.at[slot], wx_r.at[slot], *along_x(step))

    def c_copy(n, part, at):
        slot = n * 3 + part
        return send(at, at, wc_s.at[slot], wc_r.at[slot], partner, zero)

    def half_at(n, r):
        return wf.at[:, source_of(n), r, columns]

    def quarter_at(n, r, which, quarter):
        return wf.at[:, source_of(n), r, columns_of(which, quarter)]

    def pass_on(n):
        for quarter in range(2):
            copy = x_copy(n, quarter, quarter_at(n, rows, side, quarter))
            copy.start()
            sent.append(copy)
        copy = c_copy(n, 0, half_at(n, rows))
        copy.start()
        sent.append(copy)

    for n in range(len(steps_y)):
        copy = y_copy(n, half_at(0, rows))
        copy.start()
        sent.append(copy)
    pass_on(0)
    for n in range(len(steps_y)):
        y_copy(n, half_at(n + 1, rows)).wait_recv()
        pass_on(n + 1)
    for n in range(Y_LO):
        for quarter in range(2):
            at = quarter_at(n, rows, 1 - side, quarter)
            x_copy(n, quarter, at).wait_recv()
            copy = c_copy(n, 1 + quarter, at)
            copy.start()
            sent.append(copy)
    other_rows = rows_of(1 - core)
    for n in range(Y_LO):
        c_copy(n, 0, half_at(n, other_rows)).wait_recv()
        for quarter in range(2):
            c_copy(n, 1 + quarter, quarter_at(n, other_rows, 1 - side, quarter)).wait_recv()

    for h in range(HEADS):
        lanes = slice(h * HEAD, (h + 1) * HEAD)
        weight = wf[:, :, :, lanes].reshape(model, HEAD)
        feat, slope = features(dot(inp[...], weight))
        fk[:, lanes] = feat.astype(BF16)
        slk[:, lanes] = slope

    part = WIDTH // GROUP
    padded = f_out.shape[1]

    def scan_start(mats, sums, out, inside, s_sem, r_sem):
        per = HEAD // part if part <= HEAD else 1
        for h in range(HEADS):
            for p in range(per):
                slot = h * per + p
                out[slot, 0:part] = mats[h][p * part : (p + 1) * part].astype(BF16)
                out[slot, part:padded] = jnp.broadcast_to(sums[h], (padded - part, HEAD)).astype(
                    BF16
                )
        for k in range(1, GROUP):
            copy = send(
                out.at[lax.rem(own + k, GROUP)], inside.at[own],
                s_sem.at[k - 1], r_sem.at[k - 1], *in_group(k),
            )
            copy.start()
            sent.append(copy)
        inside[pl.ds(own, 1)] = out[pl.ds(own, 1)]

    def group_wait(buffer, s_sem, r_sem):
        for k in range(1, GROUP):
            at = buffer.at[lax.rem(own - k + GROUP, GROUP)]
            send(at, at, s_sem.at[k - 1], r_sem.at[k - 1], *in_group(k)).wait_recv()

    def scan_total(out, inside, total, total_in, s_sem, r_sem, y_s, y_r):
        group_wait(inside, s_sem, r_sem)
        running = wide(inside[0])
        for p in range(1, GROUP):
            running = running + wide(inside[p])
        total[...] = running.astype(BF16)
        copy = send(total, total_in, y_s.at[0], y_r.at[0], *along_y(Y_LO))
        copy.start()
        sent.append(copy)
        return copy

    def scan_back(inside, total_in, copy, taken, order, pre, ret, s_sem, r_sem):
        copy.wait_recv()
        running = wide(total_in[...]) * taken.astype(F32)
        for p in order:
            pre[p] = running.astype(BF16)
            running = running + wide(inside[p])
        for k in range(1, GROUP):
            copy = send(
                pre.at[lax.rem(own + k, GROUP)], ret.at[own],
                s_sem.at[k - 1], r_sem.at[k - 1], *in_group(k),
            )
            copy.start()
            sent.append(copy)
        ret[pl.ds(own, 1)] = pre[pl.ds(own, 1)]

    def scan_result(ret, h):
        per = HEAD // part
        mats = [ret[h * per + p, 0:part] for p in range(per)]
        mat = mats[0] if per == 1 else jnp.concatenate(mats, axis=0)
        return mat, wide(ret[h * per, part : part + 16])[0:1]

    mats, sums = [], []
    for h in range(HEADS):
        lanes = slice(h * HEAD, (h + 1) * HEAD)
        mats.append(dot_tn(fk[:, lanes], v[:, lanes]))
        sums.append(jnp.sum(wide(fk[:, lanes]), axis=0, keepdims=True))
    scan_start(mats, sums, f_out, f_in, fa_s, fa_r)

    causal = lax.broadcasted_iota(jnp.int32, (tokens, tokens), 0) >= lax.broadcasted_iota(
        jnp.int32, (tokens, tokens), 1
    )

    def inside_block(h):
        lanes = slice(h * HEAD, (h + 1) * HEAD)
        scores = dot_nt(fq[:, lanes], fk[:, lanes])
        weights = jnp.where(causal, scores, 0.0).astype(BF16)
        wts[h] = weights
        extended = jnp.concatenate([v[:, lanes], jnp.ones((tokens, HEAD), BF16)], axis=1)
        both = dot(weights, extended)
        numi[:, lanes] = both[:, :HEAD]
        deni[:, lanes] = both[:, HEAD:]

    inside_block(0)
    swap = scan_total(f_out, f_in, f_tot, f_tot_in, fa_s, fa_r, fy_s, fy_r)
    for h in range(1, HEADS - 1):
        inside_block(h)
    scan_back(f_in, f_tot_in, swap, y_hi, range(GROUP), f_pre, f_ret, fb_s, fb_r)
    inside_block(HEADS - 1)
    group_wait(f_ret, fb_s, fb_r)

    squares = jnp.zeros((tokens, HEAD), F32)
    crossed = jnp.zeros((tokens, HEAD), F32)
    for h in range(HEADS):
        lanes = slice(h * HEAD, (h + 1) * HEAD)
        prior, prior_sum = scan_result(f_ret, h)
        now = (st[h] + wide(prior)).astype(BF16)
        norm_now = nm[h : h + 1] + prior_sum
        state[h] = now
        norm[h] = norm_now
        query = fq[:, lanes]
        numerator = numi[:, lanes] + dot(query, now)
        denominator = deni[:, lanes] + jnp.sum(wide(query) * norm_now, axis=1, keepdims=True)
        inverse = 1.0 / denominator
        out = numerator * inverse
        ho[:, lanes] = out
        rec[:, lanes] = inverse
        squares = squares + out * out
        crossed = crossed + wide(og[:, lanes]) * gain[:, lanes] * out
    inv_rms = lax.rsqrt(jnp.sum(squares, axis=1, keepdims=True) / WIDTH + epsilon)
    inner = jnp.sum(crossed, axis=1, keepdims=True) / WIDTH
    factor = inner * inv_rms * inv_rms
    mats, sums = [], []
    for h in range(HEADS):
        lanes = slice(h * HEAD, (h + 1) * HEAD)
        out = ho[:, lanes]
        d_head = inv_rms * (wide(og[:, lanes]) * gain[:, lanes] - out * factor)
        numerator_grad = (d_head * rec[:, lanes]).astype(BF16)
        denominator_grad = -jnp.sum(d_head * out, axis=1, keepdims=True) * rec[:, lanes]
        gn[:, lanes] = numerator_grad
        gd[:, lanes] = denominator_grad
        mats.append(dot_tn(fq[:, lanes], numerator_grad))
        sums.append(jnp.sum(denominator_grad * wide(fq[:, lanes]), axis=0, keepdims=True))
    scan_start(mats, sums, b_out, b_in, ba_s, ba_r)

    def block_grads(h):
        lanes = slice(h * HEAD, (h + 1) * HEAD)
        grad = gn[:, lanes]
        row_grad = gd[:, lanes]
        d_weights = dot_nt(grad, v[:, lanes]) + jnp.concatenate(
            [row_grad] * (tokens // HEAD), axis=1
        )
        d_weights = jnp.where(causal, d_weights, 0.0).astype(BF16)
        dfk[:, lanes] = dot_tn(d_weights, fq[:, lanes])
        dval[:, lanes] = dot_tn(wts[h], grad)
        d_query = dot(d_weights, fk[:, lanes]) + dot_nt(grad, state[h]) + row_grad * norm[h]
        qg[:, lanes] = (d_query * slq[:, lanes]).astype(BF16)

    block_grads(0)
    swap = scan_total(b_out, b_in, b_tot, b_tot_in, ba_s, ba_r, by_s, by_r)
    for h in range(1, HEADS - 1):
        block_grads(h)
    scan_back(
        b_in, b_tot_in, swap, 1 - y_hi, range(GROUP - 1, -1, -1), b_pre, b_ret, bb_s, bb_r
    )
    for h in range(HEADS):
        lanes = slice(h * HEAD, (h + 1) * HEAD)
        att[:, lanes] = (ho[:, lanes] * inv_rms * gain[:, lanes]).astype(BF16)
    block_grads(HEADS - 1)
    group_wait(b_ret, bb_s, bb_r)
    for h in range(HEADS):
        lanes = slice(h * HEAD, (h + 1) * HEAD)
        carry, carry_sum = scan_result(b_ret, h)
        total = dfk[:, lanes] + dot_nt(v[:, lanes], carry) + carry_sum
        dk[:, lanes] = (total * slk[:, lanes]).astype(BF16)

    rows_out = Z * Y_LO

    def partial_of(xx, c):
        left = jnp.concatenate([inpt[hi, xx, c] for hi in range(Y_HI)], axis=0)
        return dot(left, dk[...])

    def rc_copy(k):
        return send(gsend.at[k], grecv.at[k], rc_s.at[k], rc_r.at[k], partner, zero)

    def rx_copy(slot):
        return send(
            xsend.at[slot], xrecv.at[slot], rx_s.at[slot], rx_r.at[slot],
            *along_x(1 if slot == 0 else X - 1),
        )

    def relay_copy(slot):
        return send(
            vsend.at[slot], vrecv.at[slot], rv_s.at[slot], rv_r.at[slot],
            *along_x(1 if slot == 0 else X - 1),
        )

    def start(copy):
        copy.start()
        sent.append(copy)

    order = (2, 1, 3, 0)
    for k in order:
        gsend[k] = partial_of(lax.rem(x + k, X), 1 - core).astype(BF16)
        start(rc_copy(k))

    def both_cores(k):
        mine = partial_of(lax.rem(x + k, X), core)
        rc_copy(k).wait_recv()
        return mine + wide(grecv[k])

    middle = rows_out
    far = both_cores(2).astype(BF16)
    vsend[0] = far[:middle]
    start(relay_copy(0))
    vsend[1] = far[middle:]
    start(relay_copy(1))
    up = both_cores(1)
    down = both_cores(3)
    relay_copy(0).wait_recv()
    xsend[0, 0:middle] = (up[:middle] + wide(vrecv[0])).astype(BF16)
    xsend[0, middle : 2 * middle] = up[middle:].astype(BF16)
    start(rx_copy(0))
    relay_copy(1).wait_recv()
    xsend[1, 0:middle] = down[:middle].astype(BF16)
    xsend[1, middle : 2 * middle] = (down[middle:] + wide(vrecv[1])).astype(BF16)
    start(rx_copy(1))
    gown[...] = both_cores(0)

    for h in range(HEADS):
        lanes = slice(h * HEAD, (h + 1) * HEAD)
        carry, _ = scan_result(b_ret, h)
        vg[:, lanes] = (dval[:, lanes] + dot(fk[:, lanes], carry)).astype(BF16)
    ig[...] = dot_nt(dk[...], wf[...].reshape(model, WIDTH)).astype(BF16)

    total = gown[...]
    for slot in range(2):
        rx_copy(slot).wait_recv()
        total = total + wide(xrecv[slot])
    for there in range(RING_Y):
        part_y = total[there * Z : (there + 1) * Z]
        ykeep[there] = part_y
        ysend[there] = part_y.astype(BF16)

    def ry_copy(k):
        return send(
            ysend.at[lax.rem(y + k, RING_Y)], yrecv.at[k - 1],
            ry_s.at[k - 1], ry_r.at[k - 1], *along_y(k),
        )

    for k in (4, 3, 5, 2, 6, 1, 7) if RING_Y == 8 else range(1, RING_Y):
        copy = ry_copy(k)
        copy.start()
        sent.append(copy)
    total = ykeep[pl.ds(y, 1)][0]
    for k in range(1, RING_Y):
        ry_copy(k).wait_recv()
        total = total + wide(yrecv[k - 1])
    zsend[:, 0, :] = total

    def rz_copy(k):
        return send(
            zsend.at[lax.rem(z + k, Z)], zrecv.at[k - 1],
            rz_s.at[k - 1], rz_r.at[k - 1], *along_z(k),
        )

    def rz_start(n, carry):
        rz_copy(far_first(n)).start()
        return carry

    lax.fori_loop(0, Z - 1, rz_start, 0)
    last = zsend[pl.ds(z, 1)][0]
    for k in range(1, Z):
        rz_copy(k).wait_recv()
        last = last + zrecv[k - 1]
    wg[...] = last

    for copy in sent:
        copy.wait_send()

    def z_sent(k, carry):
        z_copy(k).wait_send()
        rz_copy(k).wait_send()
        return carry

    lax.fori_loop(1, Z, z_sent, 0)


def shards(inputs, queries, values, w_key, state_in, norm_in, out_gain, out_grad):
    docs, tokens, model = inputs.shape
    depth = w_key.shape[0]
    part = WIDTH // GROUP
    padded = part + 16
    rows_out = Z * Y_LO
    dma = pltpu.SemaphoreType.DMA
    vmem = pltpu.VMEM
    scan_buffers = [
        vmem((GROUP, padded, HEAD), BF16),
        vmem((GROUP, padded, HEAD), BF16),
        vmem((padded, HEAD), BF16),
        vmem((padded, HEAD), BF16),
        vmem((GROUP, padded, HEAD), BF16),
        vmem((GROUP, padded, HEAD), BF16),
    ]
    scan_sems = [dma((GROUP - 1,))] * 2 + [dma((1,))] * 2 + [dma((GROUP - 1,))] * 2
    scratch = (
        [
            vmem((tokens, model), BF16),
            vmem((tokens, WIDTH), BF16),
            vmem((tokens, WIDTH), BF16),
            vmem((HEADS, HEAD, HEAD), F32),
            vmem((HEADS, HEAD), F32),
            vmem((1, WIDTH), F32),
            vmem((tokens, WIDTH), BF16),
            vmem((Z, Y_LO, depth, WIDTH), BF16),
            vmem((Y_HI, X, CORES, rows_out, tokens), BF16),
            vmem((tokens, WIDTH), BF16),
            vmem((tokens, WIDTH), F32),
            vmem((tokens, WIDTH), BF16),
            vmem((tokens, WIDTH), F32),
            vmem((HEADS, tokens, tokens), BF16),
            vmem((tokens, WIDTH), F32),
            vmem((tokens, WIDTH), F32),
            vmem((tokens, WIDTH), F32),
            vmem((tokens, WIDTH), F32),
            vmem((tokens, WIDTH), BF16),
            vmem((tokens, WIDTH), F32),
            vmem((HEADS, HEAD, HEAD), BF16),
            vmem((tokens, WIDTH), F32),
            vmem((tokens, WIDTH), F32),
            vmem((tokens, WIDTH), BF16),
            vmem((HEADS, 1, HEAD), F32),
        ]
        + scan_buffers
        + scan_buffers
        + [
            vmem((Y_HI * rows_out, WIDTH), F32),
            vmem((X, Y_HI * rows_out, WIDTH), BF16),
            vmem((X, Y_HI * rows_out, WIDTH), BF16),
            vmem((2, rows_out, WIDTH), BF16),
            vmem((2, rows_out, WIDTH), BF16),
            vmem((2, Y_HI * rows_out, WIDTH), BF16),
            vmem((2, Y_HI * rows_out, WIDTH), BF16),
            vmem((RING_Y, Z, WIDTH), F32),
            vmem((RING_Y, Z, WIDTH), BF16),
            vmem((RING_Y - 1, Z, WIDTH), BF16),
            vmem((Z, 1, WIDTH), F32),
            vmem((Z - 1, 1, WIDTH), F32),
        ]
        + [dma((1,)), dma((7,))]
        + [dma((Z - 1,))] * 2
        + [dma((Y_LO - 1,))] * 2
        + [dma((Y_LO * 2,))] * 2
        + [dma((Y_LO * 3,))] * 2
        + scan_sems
        + scan_sems
        + [dma((X,))] * 2
        + [dma((2,))] * 4
        + [dma((RING_Y - 1,))] * 2
        + [dma((Z - 1,))] * 2
    )
    space = pl.BlockSpec(memory_space=pltpu.VMEM)
    anywhere = pl.BlockSpec(memory_space=pl.ANY)
    results = (
        ((tokens, WIDTH), BF16),
        ((tokens, model), BF16),
        ((tokens, WIDTH), BF16),
        ((tokens, WIDTH), BF16),
        ((1, WIDTH), F32),
    )
    outs = pl.pallas_call(
        body,
        out_shape=tuple(pltpu.VMEM(*r) for r in results),
        in_specs=[anywhere] * 8,
        out_specs=(space,) * 5,
        scratch_shapes=scratch,
        compiler_params=pltpu.CompilerParams(
            collective_id=0, has_side_effects=True, vmem_limit_bytes=56 * 1024 * 1024
        ),
    )(
        inputs[0],
        queries[0],
        values[0],
        w_key,
        state_in[0],
        norm_in[0],
        out_gain[None],
        out_grad[0],
    )
    return (outs[0][None], outs[1][None], outs[2][None], outs[3][None], outs[4])


def solution(mesh):
    return jax.shard_map(
        shards,
        mesh=mesh,
        in_specs=(
            P("zero", "seq", None),
            P("zero", "seq", None),
            P("zero", "seq", None),
            P("zero", None),
            P("zero", None, None, None),
            P("zero", None, None),
            P(),
            P("zero", "seq", None),
        ),
        out_specs=(
            P("zero", "seq", None),
            P("zero", "seq", None),
            P("zero", "seq", None),
            P("zero", "seq", None),
            P(("seq", "zero"), None),
        ),
        check_vma=False,
    )
```

```python
import jax
import jax.numpy as jnp
from jax import lax
from jax.experimental import pallas as pl
from jax.experimental.pallas import tpu as pltpu
from jax.sharding import PartitionSpec as P

epsilon = 1e-06
MESH = pl.DeviceIdType.MESH
F32 = jnp.float32
BF16 = jnp.bfloat16

Y_HI, X, CORES = 2, 4, 2
Z, Y_LO = 16, 4
GROUP = X * CORES
RING_Y = Y_HI * Y_LO
HEADS, HEAD = 4, 128
WIDTH = HEADS * HEAD


def dot(a, b):
    return jnp.dot(a, b, preferred_element_type=F32)


def dot_nt(a, b):
    return lax.dot_general(a, b, (((1,), (1,)), ((), ())), preferred_element_type=F32)


def dot_tn(a, b):
    return lax.dot_general(a, b, (((0,), (0,)), ((), ())), preferred_element_type=F32)


def wide(value):
    return value.astype(F32)


def features(value):
    low = jnp.exp(jnp.minimum(value, 0.0))
    positive = value > 0
    return jnp.where(positive, value + 1.0, low), jnp.where(positive, 1.0, low)


def body(
    inp_hbm, q_hbm, v_hbm, w, st_hbm, nm_hbm, gain_hbm, og_hbm,
    big, ig, wg,
    inp, q, v, st, nm, gain, og,
    wf, inpt, fq, slq, fk, slk, wts, numi, deni, ho, rec, gn, gd, state, dfk, dval, dk, norm,
    f_out, f_in, f_tot, f_tot_in, f_pre, f_ret,
    b_out, b_in, b_tot, b_tot_in, b_pre, b_ret,
    gown, gsend, grecv, vsend, vrecv, xsend, xrecv, ykeep, ysend, yrecv, zsend, zrecv,
    local_sem, load_sem,
    wz_s, wz_r, wy_s, wy_r, wx_s, wx_r, wc_s, wc_r,
    fa_s, fa_r, fy_s, fy_r, fb_s, fb_r,
    ba_s, ba_r, by_s, by_r, bb_s, bb_r,
    rc_s, rc_r, rv_s, rv_r, rx_s, rx_r, ry_s, ry_r, rz_s, rz_r,
):
    att, qg, vg = big.at[0], big.at[1], big.at[2]
    seq, zero = lax.axis_index("seq"), lax.axis_index("zero")
    core = lax.rem(seq, CORES)
    x = lax.rem(seq // CORES, X)
    y_hi = seq // GROUP
    z = zero // Y_LO
    y_lo = lax.rem(zero, Y_LO)
    y = y_hi * Y_LO + y_lo
    own = x * CORES + core
    partner = seq + 1 - 2 * core
    tokens, model = inp.shape
    depth = w.shape[0]
    half = depth // CORES
    wide_block = WIDTH // 2
    block = wide_block // 2
    side = lax.rem(x, 2)

    def send(source, target, s_sem, r_sem, to_seq, to_zero):
        return pltpu.make_async_remote_copy(
            src_ref=source,
            dst_ref=target,
            send_sem=s_sem,
            recv_sem=r_sem,
            device_id={"seq": to_seq, "zero": to_zero},
            device_id_type=MESH,
        )

    def along_z(k):
        return seq, lax.rem(z + k, Z) * Y_LO + y_lo

    def along_y(k):
        there = lax.rem(y + k + RING_Y, RING_Y)
        return (
            (there // Y_LO) * GROUP + own,
            z * Y_LO + lax.rem(there, Y_LO),
        )

    def along_x(k):
        return y_hi * GROUP + lax.rem(x + k, X) * CORES + core, zero

    def in_group(k):
        return y_hi * GROUP + lax.rem(own + k, GROUP), zero

    barrier = pltpu.get_barrier_semaphore()

    def greet(place):
        pl.semaphore_signal(
            barrier, inc=1, device_id={"seq": place[0], "zero": place[1]}, device_id_type=MESH
        )

    def greet_z(k, carry):
        greet(along_z(k))
        return carry

    lax.fori_loop(1, Z, greet_z, 0)
    for k in range(1, RING_Y):
        greet(along_y(k))
    for k in range(1, GROUP):
        greet(in_group(k))
    loads = [
        pltpu.make_async_copy(outer, inner, load_sem.at[n])
        for n, (outer, inner) in enumerate(
            (
                (inp_hbm, inp), (q_hbm, q), (v_hbm, v), (st_hbm, st),
                (nm_hbm, nm), (gain_hbm, gain), (og_hbm, og),
            )
        )
    ]
    for load in loads:
        load.start()
    pl.semaphore_wait(barrier, Z + RING_Y + GROUP - 3)

    sent = []

    def settle():
        for copy in sent:
            copy.wait_send()
        sent.clear()

    def rows_of(c):
        return pl.ds(pl.multiple_of(c * half, half), half)

    def columns_of(which, quarter):
        return pl.ds(pl.multiple_of(which * wide_block + quarter * block, block), block)

    rows = rows_of(core)
    columns = pl.ds(pl.multiple_of(side * wide_block, wide_block), wide_block)

    def z_copy(k):
        return send(
            w.at[rows, columns], wf.at[z, y_lo, rows, columns],
            wz_s.at[k - 1], wz_r.at[k - 1], *along_z(k),
        )

    def z_arrival(k):
        origin = lax.rem(z - k + Z, Z)
        return send(
            w.at[rows, columns], wf.at[origin, y_lo, rows, columns],
            wz_s.at[k - 1], wz_r.at[k - 1], *along_z(k),
        )

    def far_first(n):
        return Z // 2 + ((n + 1) // 2) * (1 - 2 * lax.rem(n, 2))

    def z_start(n, carry):
        z_copy(far_first(n)).start()
        return carry

    lax.fori_loop(0, Z - 1, z_start, 0)
    keep = pltpu.make_async_copy(
        w.at[rows, columns], wf.at[z, y_lo, rows, columns], local_sem.at[0]
    )
    keep.start()

    for load in loads:
        load.wait()

    span = CORES * Z * Y_LO
    j = lax.broadcasted_iota(jnp.int32, (span, span), 0)
    i = lax.broadcasted_iota(jnp.int32, (span, span), 1)
    within = lax.rem(j, Z * Y_LO)
    source = (j - within) + lax.rem(within, Z) * Y_LO + within // Z
    pick = jnp.where(source == i, 1.0, 0.0).astype(BF16)
    for b in range(Y_HI * X):
        turned = dot_nt(pick, inp[:, b * span : (b + 1) * span]).astype(BF16)
        for c in range(CORES):
            inpt[b // X, b % X, c] = turned[c * (span // CORES) : (c + 1) * (span // CORES)]
    for h in range(HEADS):
        lanes = slice(h * HEAD, (h + 1) * HEAD)
        feat, slope = features(wide(q[:, lanes]))
        fq[:, lanes] = feat.astype(BF16)
        slq[:, lanes] = slope

    def z_wait(k, carry):
        z_arrival(k).wait_recv()
        return carry

    keep.wait()
    lax.fori_loop(1, Z, z_wait, 0)

    steps_y = [1, -1, 2 - 4 * core] if Y_LO == 4 else [1]

    def source_of(n):
        return y_lo if n == 0 else lax.rem(y_lo - steps_y[n - 1] + 2 * Y_LO, Y_LO)

    def y_copy(n, at):
        return send(at, at, wy_s.at[n], wy_r.at[n], *along_y(steps_y[n]))

    def x_copy(n, quarter, at):
        slot = n * 2 + quarter
        step = 1 if quarter == 0 else X - 1
        return send(at, at, wx_s.at[slot], wx_r.at[slot], *along_x(step))

    def c_copy(slot, at):
        return send(at, at, wc_s.at[slot], wc_r.at[slot], partner, zero)

    def other_half(n, r):
        far_columns = pl.ds(pl.multiple_of((1 - side) * wide_block, wide_block), wide_block)
        return wf.at[:, source_of(n), r, far_columns]

    def half_at(n, r):
        return wf.at[:, source_of(n), r, columns]

    def quarter_at(n, r, which, quarter):
        return wf.at[:, source_of(n), r, columns_of(which, quarter)]

    def pass_on(n):
        for quarter in range(2):
            copy = x_copy(n, quarter, quarter_at(n, rows, side, quarter))
            copy.start()
            sent.append(copy)

    for n in range(len(steps_y)):
        copy = y_copy(n, half_at(0, rows))
        copy.start()
        sent.append(copy)
    pass_on(0)
    for n in range(len(steps_y)):
        y_copy(n, half_at(n + 1, rows)).wait_recv()
        pass_on(n + 1)
    other_rows = rows_of(1 - core)

    def own_half(r):
        return wf.at[:, :, r, columns]

    copy = c_copy(0, own_half(rows))
    copy.start()
    sent.append(copy)
    for n in range(Y_LO):
        for quarter in range(2):
            x_copy(n, quarter, quarter_at(n, rows, 1 - side, quarter)).wait_recv()
        copy = c_copy(1 + n, other_half(n, rows))
        copy.start()
        sent.append(copy)
    c_copy(0, own_half(other_rows)).wait_recv()
    for n in range(Y_LO):
        c_copy(1 + n, other_half(n, other_rows)).wait_recv()

    for h in range(HEADS // 2):
        lanes = slice(h * 2 * HEAD, (h + 1) * 2 * HEAD)
        weight = wf[:, :, :, lanes].reshape(model, 2 * HEAD)
        feat, slope = features(dot(inp[...], weight))
        fk[:, lanes] = feat.astype(BF16)
        slk[:, lanes] = slope

    part = WIDTH // GROUP
    padded = f_out.shape[1]
    far_group = sorted(range(1, GROUP), key=lambda k: abs(2 * k - GROUP))

    def scan_start(mats, sums, out, inside, s_sem, r_sem):
        per = HEAD // part if part <= HEAD else 1
        for h in range(HEADS):
            for p in range(per):
                slot = h * per + p
                out[slot, 0:part] = mats[h][p * part : (p + 1) * part].astype(BF16)
                out[slot, part:padded] = jnp.broadcast_to(sums[h], (padded - part, HEAD)).astype(
                    BF16
                )
        for k in far_group:
            copy = send(
                out.at[lax.rem(own + k, GROUP)], inside.at[own],
                s_sem.at[k - 1], r_sem.at[k - 1], *in_group(k),
            )
            copy.start()
            sent.append(copy)
        inside[pl.ds(own, 1)] = out[pl.ds(own, 1)]

    def group_wait(buffer, s_sem, r_sem):
        for k in range(1, GROUP):
            at = buffer.at[lax.rem(own - k + GROUP, GROUP)]
            send(at, at, s_sem.at[k - 1], r_sem.at[k - 1], *in_group(k)).wait_recv()

    def scan_total(out, inside, total, total_in, s_sem, r_sem, y_s, y_r):
        group_wait(inside, s_sem, r_sem)
        running = wide(inside[0])
        for p in range(1, GROUP):
            running = running + wide(inside[p])
        total[...] = running.astype(BF16)
        copy = send(total, total_in, y_s.at[0], y_r.at[0], *along_y(Y_LO))
        copy.start()
        sent.append(copy)
        return copy

    def scan_back(inside, total_in, copy, taken, order, pre, ret, s_sem, r_sem):
        copy.wait_recv()
        running = wide(total_in[...]) * taken.astype(F32)
        for p in order:
            pre[p] = running.astype(BF16)
            running = running + wide(inside[p])
        for k in far_group:
            copy = send(
                pre.at[lax.rem(own + k, GROUP)], ret.at[own],
                s_sem.at[k - 1], r_sem.at[k - 1], *in_group(k),
            )
            copy.start()
            sent.append(copy)
        ret[pl.ds(own, 1)] = pre[pl.ds(own, 1)]

    def scan_result(ret, h):
        per = HEAD // part
        mats = [ret[h * per + p, 0:part] for p in range(per)]
        mat = mats[0] if per == 1 else jnp.concatenate(mats, axis=0)
        return mat, wide(ret[h * per, part : part + 8])[0:1]

    mats, sums = [], []
    for h in range(HEADS):
        lanes = slice(h * HEAD, (h + 1) * HEAD)
        mats.append(dot_tn(fk[:, lanes], v[:, lanes]))
        sums.append(jnp.sum(wide(fk[:, lanes]), axis=0, keepdims=True))
    scan_start(mats, sums, f_out, f_in, fa_s, fa_r)

    causal = lax.broadcasted_iota(jnp.int32, (tokens, tokens), 0) >= lax.broadcasted_iota(
        jnp.int32, (tokens, tokens), 1
    )

    def inside_block(h):
        lanes = slice(h * HEAD, (h + 1) * HEAD)
        scores = dot_nt(fq[:, lanes], fk[:, lanes])
        weights = jnp.where(causal, scores, 0.0).astype(BF16)
        wts[h] = weights
        extended = jnp.concatenate([v[:, lanes], jnp.ones((tokens, HEAD), BF16)], axis=1)
        both = dot(weights, extended)
        numi[:, lanes] = both[:, :HEAD]
        deni[:, lanes] = both[:, HEAD:]

    inside_block(0)
    swap = scan_total(f_out, f_in, f_tot, f_tot_in, fa_s, fa_r, fy_s, fy_r)
    for h in range(1, HEADS - 1):
        inside_block(h)
    scan_back(f_in, f_tot_in, swap, y_hi, range(GROUP), f_pre, f_ret, fb_s, fb_r)
    inside_block(HEADS - 1)
    group_wait(f_ret, fb_s, fb_r)

    squares = jnp.zeros((tokens, HEAD), F32)
    crossed = jnp.zeros((tokens, HEAD), F32)
    for h in range(HEADS):
        lanes = slice(h * HEAD, (h + 1) * HEAD)
        prior, prior_sum = scan_result(f_ret, h)
        now = (st[h] + wide(prior)).astype(BF16)
        norm_now = nm[h : h + 1] + prior_sum
        state[h] = now
        norm[h] = norm_now
        query = fq[:, lanes]
        numerator = numi[:, lanes] + dot(query, now)
        denominator = deni[:, lanes] + jnp.sum(wide(query) * norm_now, axis=1, keepdims=True)
        inverse = 1.0 / denominator
        out = numerator * inverse
        ho[:, lanes] = out
        rec[:, lanes] = inverse
        squares = squares + out * out
        crossed = crossed + wide(og[:, lanes]) * gain[:, lanes] * out
    inv_rms = lax.rsqrt(jnp.sum(squares, axis=1, keepdims=True) / WIDTH + epsilon)
    inner = jnp.sum(crossed, axis=1, keepdims=True) / WIDTH
    factor = inner * inv_rms * inv_rms
    mats, sums = [], []
    for h in range(HEADS):
        lanes = slice(h * HEAD, (h + 1) * HEAD)
        out = ho[:, lanes]
        d_head = inv_rms * (wide(og[:, lanes]) * gain[:, lanes] - out * factor)
        numerator_grad = (d_head * rec[:, lanes]).astype(BF16)
        denominator_grad = -jnp.sum(d_head * out, axis=1, keepdims=True) * rec[:, lanes]
        gn[:, lanes] = numerator_grad
        gd[:, lanes] = denominator_grad
        mats.append(dot_tn(fq[:, lanes], numerator_grad))
        sums.append(jnp.sum(denominator_grad * wide(fq[:, lanes]), axis=0, keepdims=True))
    scan_start(mats, sums, b_out, b_in, ba_s, ba_r)

    def block_grads(h):
        lanes = slice(h * HEAD, (h + 1) * HEAD)
        grad = gn[:, lanes]
        row_grad = gd[:, lanes]
        d_weights = dot_nt(grad, v[:, lanes]) + jnp.concatenate(
            [row_grad] * (tokens // HEAD), axis=1
        )
        d_weights = jnp.where(causal, d_weights, 0.0).astype(BF16)
        dfk[:, lanes] = dot_tn(d_weights, fq[:, lanes])
        dval[:, lanes] = dot_tn(wts[h], grad)
        d_query = dot(d_weights, fk[:, lanes]) + dot_nt(grad, state[h]) + row_grad * norm[h]
        qg[:, lanes] = (d_query * slq[:, lanes]).astype(BF16)

    block_grads(0)
    swap = scan_total(b_out, b_in, b_tot, b_tot_in, ba_s, ba_r, by_s, by_r)
    for h in range(1, HEADS - 1):
        block_grads(h)
    scan_back(
        b_in, b_tot_in, swap, 1 - y_hi, range(GROUP - 1, -1, -1), b_pre, b_ret, bb_s, bb_r
    )
    for h in range(HEADS):
        lanes = slice(h * HEAD, (h + 1) * HEAD)
        att[:, lanes] = (ho[:, lanes] * inv_rms * gain[:, lanes]).astype(BF16)
    block_grads(HEADS - 1)
    group_wait(b_ret, bb_s, bb_r)
    for h in range(HEADS):
        lanes = slice(h * HEAD, (h + 1) * HEAD)
        carry, carry_sum = scan_result(b_ret, h)
        total = dfk[:, lanes] + dot_nt(v[:, lanes], carry) + carry_sum
        dk[:, lanes] = (total * slk[:, lanes]).astype(BF16)

    rows_out = Z * Y_LO

    def partial_of(xx, c):
        left = jnp.concatenate([inpt[hi, xx, c] for hi in range(Y_HI)], axis=0)
        return dot(left, dk[...])

    def rc_copy(k):
        return send(gsend.at[k], grecv.at[k], rc_s.at[k], rc_r.at[k], partner, zero)

    def rx_copy(slot):
        return send(
            xsend.at[slot], xrecv.at[slot], rx_s.at[slot], rx_r.at[slot],
            *along_x(1 if slot == 0 else X - 1),
        )

    def relay_copy(slot):
        return send(
            vsend.at[slot], vrecv.at[slot], rv_s.at[slot], rv_r.at[slot],
            *along_x(1 if slot == 0 else X - 1),
        )

    def start(copy):
        copy.start()
        sent.append(copy)

    order = (2, 1, 3, 0)
    for k in order:
        gsend[k] = partial_of(lax.rem(x + k, X), 1 - core).astype(BF16)
        start(rc_copy(k))

    def both_cores(k):
        mine = partial_of(lax.rem(x + k, X), core)
        rc_copy(k).wait_recv()
        return mine + wide(grecv[k])

    middle = rows_out
    far = both_cores(2).astype(BF16)
    vsend[0] = far[:middle]
    start(relay_copy(0))
    vsend[1] = far[middle:]
    start(relay_copy(1))
    up = both_cores(1)
    down = both_cores(3)
    relay_copy(0).wait_recv()
    xsend[0, 0:middle] = (up[:middle] + wide(vrecv[0])).astype(BF16)
    xsend[0, middle : 2 * middle] = up[middle:].astype(BF16)
    start(rx_copy(0))
    relay_copy(1).wait_recv()
    xsend[1, 0:middle] = down[:middle].astype(BF16)
    xsend[1, middle : 2 * middle] = (down[middle:] + wide(vrecv[1])).astype(BF16)
    start(rx_copy(1))
    gown[...] = both_cores(0)

    for h in range(HEADS):
        lanes = slice(h * HEAD, (h + 1) * HEAD)
        carry, _ = scan_result(b_ret, h)
        vg[:, lanes] = (dval[:, lanes] + dot(fk[:, lanes], carry)).astype(BF16)
    ig[...] = dot_nt(dk[...], wf[...].reshape(model, WIDTH)).astype(BF16)

    settle()

    def z_sent(k, carry):
        z_copy(k).wait_send()
        return carry

    lax.fori_loop(1, Z, z_sent, 0)
    total = gown[...]
    for slot in range(2):
        rx_copy(slot).wait_recv()
        total = total + wide(xrecv[slot])
    for there in range(RING_Y):
        part_y = total[there * Z : (there + 1) * Z]
        ykeep[there] = part_y
        ysend[there] = part_y.astype(BF16)

    def ry_copy(k):
        return send(
            ysend.at[lax.rem(y + k, RING_Y)], yrecv.at[k - 1],
            ry_s.at[k - 1], ry_r.at[k - 1], *along_y(k),
        )

    for k in (4, 3, 5, 2, 6, 1, 7) if RING_Y == 8 else range(1, RING_Y):
        copy = ry_copy(k)
        copy.start()
        sent.append(copy)
    total = ykeep[pl.ds(y, 1)][0]
    for k in range(1, RING_Y):
        ry_copy(k).wait_recv()
        total = total + wide(yrecv[k - 1])
    zsend[:, 0, :] = total

    def rz_copy(k):
        return send(
            zsend.at[lax.rem(z + k, Z)], zrecv.at[k - 1],
            rz_s.at[k - 1], rz_r.at[k - 1], *along_z(k),
        )

    def rz_start(n, carry):
        rz_copy(far_first(n)).start()
        return carry

    lax.fori_loop(0, Z - 1, rz_start, 0)
    settle()
    last = zsend[pl.ds(z, 1)][0]
    for k in range(1, Z):
        rz_copy(k).wait_recv()
        last = last + zrecv[k - 1]
    wg[...] = last

    def rz_sent(k, carry):
        rz_copy(k).wait_send()
        return carry

    lax.fori_loop(1, Z, rz_sent, 0)


def shards(inputs, queries, values, w_key, state_in, norm_in, out_gain, out_grad):
    docs, tokens, model = inputs.shape
    depth = w_key.shape[0]
    part = WIDTH // GROUP
    padded = part + 8
    rows_out = Z * Y_LO
    dma = pltpu.SemaphoreType.DMA
    vmem = pltpu.VMEM
    scan_buffers = [
        vmem((GROUP, padded, HEAD), BF16),
        vmem((GROUP, padded, HEAD), BF16),
        vmem((padded, HEAD), BF16),
        vmem((padded, HEAD), BF16),
        vmem((GROUP, padded, HEAD), BF16),
        vmem((GROUP, padded, HEAD), BF16),
    ]
    scan_sems = [dma((GROUP - 1,))] * 2 + [dma((1,))] * 2 + [dma((GROUP - 1,))] * 2
    scratch = (
        [
            vmem((tokens, model), BF16),
            vmem((tokens, WIDTH), BF16),
            vmem((tokens, WIDTH), BF16),
            vmem((HEADS, HEAD, HEAD), F32),
            vmem((HEADS, HEAD), F32),
            vmem((1, WIDTH), F32),
            vmem((tokens, WIDTH), BF16),
            vmem((Z, Y_LO, depth, WIDTH), BF16),
            vmem((Y_HI, X, CORES, rows_out, tokens), BF16),
            vmem((tokens, WIDTH), BF16),
            vmem((tokens, WIDTH), F32),
            vmem((tokens, WIDTH), BF16),
            vmem((tokens, WIDTH), F32),
            vmem((HEADS, tokens, tokens), BF16),
            vmem((tokens, WIDTH), F32),
            vmem((tokens, WIDTH), F32),
            vmem((tokens, WIDTH), F32),
            vmem((tokens, WIDTH), F32),
            vmem((tokens, WIDTH), BF16),
            vmem((tokens, WIDTH), F32),
            vmem((HEADS, HEAD, HEAD), BF16),
            vmem((tokens, WIDTH), F32),
            vmem((tokens, WIDTH), F32),
            vmem((tokens, WIDTH), BF16),
            vmem((HEADS, 1, HEAD), F32),
        ]
        + scan_buffers
        + scan_buffers
        + [
            vmem((Y_HI * rows_out, WIDTH), F32),
            vmem((X, Y_HI * rows_out, WIDTH), BF16),
            vmem((X, Y_HI * rows_out, WIDTH), BF16),
            vmem((2, rows_out, WIDTH), BF16),
            vmem((2, rows_out, WIDTH), BF16),
            vmem((2, Y_HI * rows_out, WIDTH), BF16),
            vmem((2, Y_HI * rows_out, WIDTH), BF16),
            vmem((RING_Y, Z, WIDTH), F32),
            vmem((RING_Y, Z, WIDTH), BF16),
            vmem((RING_Y - 1, Z, WIDTH), BF16),
            vmem((Z, 1, WIDTH), F32),
            vmem((Z - 1, 1, WIDTH), F32),
        ]
        + [dma((1,)), dma((7,))]
        + [dma((Z - 1,))] * 2
        + [dma((Y_LO - 1,))] * 2
        + [dma((Y_LO * 2,))] * 2
        + [dma((Y_LO + 1,))] * 2
        + scan_sems
        + scan_sems
        + [dma((X,))] * 2
        + [dma((2,))] * 4
        + [dma((RING_Y - 1,))] * 2
        + [dma((Z - 1,))] * 2
    )
    space = pl.BlockSpec(memory_space=pltpu.VMEM)
    anywhere = pl.BlockSpec(memory_space=pl.ANY)
    results = (
        ((3, tokens, WIDTH), BF16),
        ((tokens, model), BF16),
        ((1, WIDTH), F32),
    )
    outs = pl.pallas_call(
        body,
        out_shape=tuple(pltpu.VMEM(*r) for r in results),
        in_specs=[anywhere] * 8,
        out_specs=(space,) * 3,
        scratch_shapes=scratch,
        compiler_params=pltpu.CompilerParams(
            collective_id=0, has_side_effects=True, vmem_limit_bytes=56 * 1024 * 1024
        ),
    )(
        inputs[0],
        queries[0],
        values[0],
        w_key,
        state_in[0],
        norm_in[0],
        out_gain[None],
        out_grad[0],
    )
    big, inputs_grad, key_grad = outs
    return (big[0:1], inputs_grad[None], big[1:2], big[2:3], key_grad)


def solution(mesh):
    return jax.shard_map(
        shards,
        mesh=mesh,
        in_specs=(
            P("zero", "seq", None),
            P("zero", "seq", None),
            P("zero", "seq", None),
            P("zero", None),
            P("zero", None, None, None),
            P("zero", None, None),
            P(),
            P("zero", "seq", None),
        ),
        out_specs=(
            P("zero", "seq", None),
            P("zero", "seq", None),
            P("zero", "seq", None),
            P("zero", "seq", None),
            P(("seq", "zero"), None),
        ),
        check_vma=False,
    )
```

```python
import jax
import jax.numpy as jnp
from jax import lax
from jax.experimental import pallas as pl
from jax.experimental.pallas import tpu as pltpu
from jax.sharding import PartitionSpec as P

epsilon = 1e-06
MESH = pl.DeviceIdType.MESH
F32 = jnp.float32
BF16 = jnp.bfloat16

Y_HI, X, CORES = 2, 4, 2
Z, Y_LO = 16, 4
GROUP = X * CORES
RING_Y = Y_HI * Y_LO
HEADS, HEAD = 4, 128
WIDTH = HEADS * HEAD


def dot(a, b):
    return jnp.dot(a, b, preferred_element_type=F32)


def dot_nt(a, b):
    return lax.dot_general(a, b, (((1,), (1,)), ((), ())), preferred_element_type=F32)


def dot_tn(a, b):
    return lax.dot_general(a, b, (((0,), (0,)), ((), ())), preferred_element_type=F32)


def wide(value):
    return value.astype(F32)


def features(value):
    low = jnp.exp(jnp.minimum(value, 0.0))
    positive = value > 0
    return jnp.where(positive, value + 1.0, low), jnp.where(positive, 1.0, low)


def body(
    inp_hbm, q_hbm, v_hbm, w, st_hbm, nm_hbm, gain_hbm, og_hbm,
    big, ig, wg,
    inp, q, v, st, nm, gain, og,
    wf, inpt, fq, slq, fk, slk, wts, numi, deni, ho, rec, gn, gd, state, dfk, dval, dk, norm,
    f_out, f_in, f_tot, f_tot_in, f_pre, f_ret,
    b_out, b_in, b_tot, b_tot_in, b_pre, b_ret,
    gown, gsend, grecv, vsend, vrecv, xsend, xrecv, ykeep, ysend, yrecv, zsend, zrecv,
    local_sem, load_sem,
    wz_s, wz_r, wy_s, wy_r, wx_s, wx_r, wc_s, wc_r,
    fa_s, fa_r, fy_s, fy_r, fb_s, fb_r,
    ba_s, ba_r, by_s, by_r, bb_s, bb_r,
    rc_s, rc_r, rv_s, rv_r, rx_s, rx_r, ry_s, ry_r, rz_s, rz_r,
):
    att, qg, vg = big.at[0], big.at[1], big.at[2]
    seq, zero = lax.axis_index("seq"), lax.axis_index("zero")
    core = lax.rem(seq, CORES)
    x = lax.rem(seq // CORES, X)
    y_hi = seq // GROUP
    z = zero // Y_LO
    y_lo = lax.rem(zero, Y_LO)
    y = y_hi * Y_LO + y_lo
    own = x * CORES + core
    partner = seq + 1 - 2 * core
    tokens, model = inp.shape
    depth = w.shape[0]
    half = depth // CORES
    wide_block = WIDTH // 2
    block = wide_block // 2
    side = lax.rem(x, 2)

    def send(source, target, s_sem, r_sem, to_seq, to_zero):
        return pltpu.make_async_remote_copy(
            src_ref=source,
            dst_ref=target,
            send_sem=s_sem,
            recv_sem=r_sem,
            device_id={"seq": to_seq, "zero": to_zero},
            device_id_type=MESH,
        )

    def along_z(k):
        return seq, lax.rem(z + k, Z) * Y_LO + y_lo

    def along_y(k):
        there = lax.rem(y + k + RING_Y, RING_Y)
        return (
            (there // Y_LO) * GROUP + own,
            z * Y_LO + lax.rem(there, Y_LO),
        )

    def along_x(k):
        return y_hi * GROUP + lax.rem(x + k, X) * CORES + core, zero

    def in_group(k):
        return y_hi * GROUP + lax.rem(own + k, GROUP), zero

    barrier = pltpu.get_barrier_semaphore()

    def greet(place):
        pl.semaphore_signal(
            barrier, inc=1, device_id={"seq": place[0], "zero": place[1]}, device_id_type=MESH
        )

    def greet_z(k, carry):
        greet(along_z(k))
        return carry

    lax.fori_loop(1, Z, greet_z, 0)
    for k in range(1, RING_Y):
        greet(along_y(k))
    for k in range(1, GROUP):
        greet(in_group(k))
    loads = [
        pltpu.make_async_copy(outer, inner, load_sem.at[n])
        for n, (outer, inner) in enumerate(
            (
                (inp_hbm, inp), (q_hbm, q), (v_hbm, v), (st_hbm, st),
                (nm_hbm, nm), (gain_hbm, gain), (og_hbm, og),
            )
        )
    ]
    for load in loads:
        load.start()
    pl.semaphore_wait(barrier, Z + RING_Y + GROUP - 3)

    sent = []

    def settle():
        for copy in sent:
            copy.wait_send()
        sent.clear()

    def rows_of(c):
        return pl.ds(pl.multiple_of(c * half, half), half)

    def columns_of(which, quarter):
        return pl.ds(pl.multiple_of(which * wide_block + quarter * block, block), block)

    rows = rows_of(core)
    columns = pl.ds(pl.multiple_of(side * wide_block, wide_block), wide_block)

    def z_copy(k):
        return send(
            w.at[rows, columns], wf.at[z, y_lo, rows, columns],
            wz_s.at[k - 1], wz_r.at[k - 1], *along_z(k),
        )

    def z_arrival(k):
        origin = lax.rem(z - k + Z, Z)
        return send(
            w.at[rows, columns], wf.at[origin, y_lo, rows, columns],
            wz_s.at[k - 1], wz_r.at[k - 1], *along_z(k),
        )

    def far_first(n):
        return Z // 2 + ((n + 1) // 2) * (1 - 2 * lax.rem(n, 2))

    def z_start(n, carry):
        z_copy(far_first(n)).start()
        return carry

    lax.fori_loop(0, Z - 1, z_start, 0)
    keep = pltpu.make_async_copy(
        w.at[rows, columns], wf.at[z, y_lo, rows, columns], local_sem.at[0]
    )
    keep.start()

    for load in loads:
        load.wait()

    span = CORES * Z * Y_LO
    j = lax.broadcasted_iota(jnp.int32, (span, span), 0)
    i = lax.broadcasted_iota(jnp.int32, (span, span), 1)
    within = lax.rem(j, Z * Y_LO)
    source = (j - within) + lax.rem(within, Z) * Y_LO + within // Z
    pick = jnp.where(source == i, 1.0, 0.0).astype(BF16)
    for b in range(Y_HI * X):
        turned = dot_nt(pick, inp[:, b * span : (b + 1) * span]).astype(BF16)
        for c in range(CORES):
            inpt[b // X, b % X, c] = turned[c * (span // CORES) : (c + 1) * (span // CORES)]
    for h in range(HEADS):
        lanes = slice(h * HEAD, (h + 1) * HEAD)
        feat, slope = features(wide(q[:, lanes]))
        fq[:, lanes] = feat.astype(BF16)
        slq[:, lanes] = slope

    def z_wait(k, carry):
        z_arrival(k).wait_recv()
        return carry

    keep.wait()
    lax.fori_loop(1, Z, z_wait, 0)

    steps_y = [1, -1, 2 - 4 * core] if Y_LO == 4 else [1]

    def source_of(n):
        return y_lo if n == 0 else lax.rem(y_lo - steps_y[n - 1] + 2 * Y_LO, Y_LO)

    def x_copy(n, quarter, at):
        slot = n * 2 + quarter
        step = 1 if quarter == 0 else X - 1
        return send(at, at, wx_s.at[slot], wx_r.at[slot], *along_x(step))

    def c_copy(slot, at):
        return send(at, at, wc_s.at[slot], wc_r.at[slot], partner, zero)

    def other_half(n, r):
        far_columns = pl.ds(pl.multiple_of((1 - side) * wide_block, wide_block), wide_block)
        return wf.at[:, source_of(n), r, far_columns]

    def half_at(n, r):
        return wf.at[:, source_of(n), r, columns]

    def quarter_at(n, r, which, quarter):
        return wf.at[:, source_of(n), r, columns_of(which, quarter)]

    def pass_on(n):
        for quarter in range(2):
            copy = x_copy(n, quarter, quarter_at(n, rows, side, quarter))
            copy.start()
            sent.append(copy)

    def y_quarter(n, quarter, at):
        slot = n * 2 + quarter
        return send(at, at, wy_s.at[slot], wy_r.at[slot], *along_y(steps_y[n]))

    for quarter in range(2):
        for n in range(len(steps_y)):
            copy = y_quarter(n, quarter, quarter_at(0, rows, side, quarter))
            copy.start()
            sent.append(copy)
    pass_on(0)
    for quarter in range(2):
        for n in range(len(steps_y)):
            at = quarter_at(n + 1, rows, side, quarter)
            y_quarter(n, quarter, at).wait_recv()
            copy = x_copy(n + 1, quarter, at)
            copy.start()
            sent.append(copy)
    other_rows = rows_of(1 - core)

    def own_half(r):
        return wf.at[:, :, r, columns]

    copy = c_copy(0, own_half(rows))
    copy.start()
    sent.append(copy)
    for n in range(Y_LO):
        for quarter in range(2):
            x_copy(n, quarter, quarter_at(n, rows, 1 - side, quarter)).wait_recv()
        copy = c_copy(1 + n, other_half(n, rows))
        copy.start()
        sent.append(copy)
    c_copy(0, own_half(other_rows)).wait_recv()
    for n in range(Y_LO):
        c_copy(1 + n, other_half(n, other_rows)).wait_recv()

    for h in range(HEADS // 2):
        lanes = slice(h * 2 * HEAD, (h + 1) * 2 * HEAD)
        weight = wf[:, :, :, lanes].reshape(model, 2 * HEAD)
        feat, slope = features(dot(inp[...], weight))
        fk[:, lanes] = feat.astype(BF16)
        slk[:, lanes] = slope

    part = WIDTH // GROUP
    padded = f_out.shape[1]
    far_group = sorted(range(1, GROUP), key=lambda k: abs(2 * k - GROUP))

    def scan_start(mats, sums, out, inside, s_sem, r_sem):
        per = HEAD // part if part <= HEAD else 1
        for h in range(HEADS):
            for p in range(per):
                slot = h * per + p
                out[slot, 0:part] = mats[h][p * part : (p + 1) * part].astype(BF16)
                out[slot, part:padded] = jnp.broadcast_to(sums[h], (padded - part, HEAD)).astype(
                    BF16
                )
        for k in far_group:
            copy = send(
                out.at[lax.rem(own + k, GROUP)], inside.at[own],
                s_sem.at[k - 1], r_sem.at[k - 1], *in_group(k),
            )
            copy.start()
            sent.append(copy)
        inside[pl.ds(own, 1)] = out[pl.ds(own, 1)]

    def group_wait(buffer, s_sem, r_sem):
        for k in range(1, GROUP):
            at = buffer.at[lax.rem(own - k + GROUP, GROUP)]
            send(at, at, s_sem.at[k - 1], r_sem.at[k - 1], *in_group(k)).wait_recv()

    def scan_total(out, inside, total, total_in, s_sem, r_sem, y_s, y_r):
        group_wait(inside, s_sem, r_sem)
        running = wide(inside[0])
        for p in range(1, GROUP):
            running = running + wide(inside[p])
        total[...] = running.astype(BF16)
        copy = send(total, total_in, y_s.at[0], y_r.at[0], *along_y(Y_LO))
        copy.start()
        sent.append(copy)
        return copy

    def scan_back(inside, total_in, copy, taken, order, pre, ret, s_sem, r_sem):
        copy.wait_recv()
        running = wide(total_in[...]) * taken.astype(F32)
        for p in order:
            pre[p] = running.astype(BF16)
            running = running + wide(inside[p])
        for k in far_group:
            copy = send(
                pre.at[lax.rem(own + k, GROUP)], ret.at[own],
                s_sem.at[k - 1], r_sem.at[k - 1], *in_group(k),
            )
            copy.start()
            sent.append(copy)
        ret[pl.ds(own, 1)] = pre[pl.ds(own, 1)]

    def scan_result(ret, h):
        per = HEAD // part
        mats = [ret[h * per + p, 0:part] for p in range(per)]
        mat = mats[0] if per == 1 else jnp.concatenate(mats, axis=0)
        return mat, wide(ret[h * per, part : part + 8])[0:1]

    mats, sums = [], []
    for h in range(HEADS):
        lanes = slice(h * HEAD, (h + 1) * HEAD)
        mats.append(dot_tn(fk[:, lanes], v[:, lanes]))
        sums.append(jnp.sum(wide(fk[:, lanes]), axis=0, keepdims=True))
    scan_start(mats, sums, f_out, f_in, fa_s, fa_r)

    causal = lax.broadcasted_iota(jnp.int32, (tokens, tokens), 0) >= lax.broadcasted_iota(
        jnp.int32, (tokens, tokens), 1
    )

    def inside_block(h):
        lanes = slice(h * HEAD, (h + 1) * HEAD)
        scores = dot_nt(fq[:, lanes], fk[:, lanes])
        weights = jnp.where(causal, scores, 0.0).astype(BF16)
        wts[h] = weights
        extended = jnp.concatenate([v[:, lanes], jnp.ones((tokens, HEAD), BF16)], axis=1)
        both = dot(weights, extended)
        numi[:, lanes] = both[:, :HEAD]
        deni[:, lanes] = both[:, HEAD:]

    swap = scan_total(f_out, f_in, f_tot, f_tot_in, fa_s, fa_r, fy_s, fy_r)
    for h in range(HEADS - 2):
        inside_block(h)
    scan_back(f_in, f_tot_in, swap, y_hi, range(GROUP), f_pre, f_ret, fb_s, fb_r)
    for h in range(HEADS - 2, HEADS):
        inside_block(h)
    group_wait(f_ret, fb_s, fb_r)

    squares = jnp.zeros((tokens, HEAD), F32)
    crossed = jnp.zeros((tokens, HEAD), F32)
    for h in range(HEADS):
        lanes = slice(h * HEAD, (h + 1) * HEAD)
        prior, prior_sum = scan_result(f_ret, h)
        now = (st[h] + wide(prior)).astype(BF16)
        norm_now = nm[h : h + 1] + prior_sum
        state[h] = now
        norm[h] = norm_now
        query = fq[:, lanes]
        numerator = numi[:, lanes] + dot(query, now)
        denominator = deni[:, lanes] + jnp.sum(wide(query) * norm_now, axis=1, keepdims=True)
        inverse = 1.0 / denominator
        out = numerator * inverse
        ho[:, lanes] = out
        rec[:, lanes] = inverse
        squares = squares + out * out
        crossed = crossed + wide(og[:, lanes]) * gain[:, lanes] * out
    inv_rms = lax.rsqrt(jnp.sum(squares, axis=1, keepdims=True) / WIDTH + epsilon)
    inner = jnp.sum(crossed, axis=1, keepdims=True) / WIDTH
    factor = inner * inv_rms * inv_rms
    mats, sums = [], []
    for h in range(HEADS):
        lanes = slice(h * HEAD, (h + 1) * HEAD)
        out = ho[:, lanes]
        d_head = inv_rms * (wide(og[:, lanes]) * gain[:, lanes] - out * factor)
        numerator_grad = (d_head * rec[:, lanes]).astype(BF16)
        denominator_grad = -jnp.sum(d_head * out, axis=1, keepdims=True) * rec[:, lanes]
        gn[:, lanes] = numerator_grad
        gd[:, lanes] = denominator_grad
        mats.append(dot_tn(fq[:, lanes], numerator_grad))
        sums.append(jnp.sum(denominator_grad * wide(fq[:, lanes]), axis=0, keepdims=True))
    scan_start(mats, sums, b_out, b_in, ba_s, ba_r)

    def block_grads(h):
        lanes = slice(h * HEAD, (h + 1) * HEAD)
        grad = gn[:, lanes]
        row_grad = gd[:, lanes]
        d_weights = dot_nt(grad, v[:, lanes]) + jnp.concatenate(
            [row_grad] * (tokens // HEAD), axis=1
        )
        d_weights = jnp.where(causal, d_weights, 0.0).astype(BF16)
        dfk[:, lanes] = dot_tn(d_weights, fq[:, lanes])
        dval[:, lanes] = dot_tn(wts[h], grad)
        d_query = dot(d_weights, fk[:, lanes]) + dot_nt(grad, state[h]) + row_grad * norm[h]
        qg[:, lanes] = (d_query * slq[:, lanes]).astype(BF16)

    swap = scan_total(b_out, b_in, b_tot, b_tot_in, ba_s, ba_r, by_s, by_r)
    for h in range(HEADS - 2):
        block_grads(h)
    scan_back(
        b_in, b_tot_in, swap, 1 - y_hi, range(GROUP - 1, -1, -1), b_pre, b_ret, bb_s, bb_r
    )
    for h in range(HEADS):
        lanes = slice(h * HEAD, (h + 1) * HEAD)
        att[:, lanes] = (ho[:, lanes] * inv_rms * gain[:, lanes]).astype(BF16)
    for h in range(HEADS - 2, HEADS):
        block_grads(h)
    group_wait(b_ret, bb_s, bb_r)
    for h in range(HEADS):
        lanes = slice(h * HEAD, (h + 1) * HEAD)
        carry, carry_sum = scan_result(b_ret, h)
        total = dfk[:, lanes] + dot_nt(v[:, lanes], carry) + carry_sum
        dk[:, lanes] = (total * slk[:, lanes]).astype(BF16)

    rows_out = Z * Y_LO

    def partial_of(xx, c):
        left = jnp.concatenate([inpt[hi, xx, c] for hi in range(Y_HI)], axis=0)
        return dot(left, dk[...])

    def rc_copy(k):
        return send(gsend.at[k], grecv.at[k], rc_s.at[k], rc_r.at[k], partner, zero)

    def rx_copy(slot):
        return send(
            xsend.at[slot], xrecv.at[slot], rx_s.at[slot], rx_r.at[slot],
            *along_x(1 if slot == 0 else X - 1),
        )

    def relay_copy(slot):
        return send(
            vsend.at[slot], vrecv.at[slot], rv_s.at[slot], rv_r.at[slot],
            *along_x(1 if slot == 0 else X - 1),
        )

    def start(copy):
        copy.start()
        sent.append(copy)

    order = (2, 1, 3, 0)
    for k in order:
        gsend[k] = partial_of(lax.rem(x + k, X), 1 - core).astype(BF16)
        start(rc_copy(k))

    def both_cores(k):
        mine = partial_of(lax.rem(x + k, X), core)
        rc_copy(k).wait_recv()
        return mine + wide(grecv[k])

    middle = rows_out
    far = both_cores(2).astype(BF16)
    vsend[0] = far[:middle]
    start(relay_copy(0))
    vsend[1] = far[middle:]
    start(relay_copy(1))
    up = both_cores(1)
    down = both_cores(3)
    relay_copy(0).wait_recv()
    xsend[0, 0:middle] = (up[:middle] + wide(vrecv[0])).astype(BF16)
    xsend[0, middle : 2 * middle] = up[middle:].astype(BF16)
    start(rx_copy(0))
    relay_copy(1).wait_recv()
    xsend[1, 0:middle] = down[:middle].astype(BF16)
    xsend[1, middle : 2 * middle] = (down[middle:] + wide(vrecv[1])).astype(BF16)
    start(rx_copy(1))
    gown[...] = both_cores(0)

    for h in range(HEADS):
        lanes = slice(h * HEAD, (h + 1) * HEAD)
        carry, _ = scan_result(b_ret, h)
        vg[:, lanes] = (dval[:, lanes] + dot(fk[:, lanes], carry)).astype(BF16)
    ig[...] = dot_nt(dk[...], wf[...].reshape(model, WIDTH)).astype(BF16)

    settle()

    def z_sent(k, carry):
        z_copy(k).wait_send()
        return carry

    lax.fori_loop(1, Z, z_sent, 0)
    total = gown[...]
    for slot in range(2):
        rx_copy(slot).wait_recv()
        total = total + wide(xrecv[slot])
    for there in range(RING_Y):
        part_y = total[there * Z : (there + 1) * Z]
        ykeep[there] = part_y
        ysend[there] = part_y.astype(BF16)

    def ry_copy(k):
        return send(
            ysend.at[lax.rem(y + k, RING_Y)], yrecv.at[k - 1],
            ry_s.at[k - 1], ry_r.at[k - 1], *along_y(k),
        )

    for k in (4, 3, 5, 2, 6, 1, 7) if RING_Y == 8 else range(1, RING_Y):
        copy = ry_copy(k)
        copy.start()
        sent.append(copy)
    total = ykeep[pl.ds(y, 1)][0]
    for k in range(1, RING_Y):
        ry_copy(k).wait_recv()
        total = total + wide(yrecv[k - 1])
    zsend[:, 0, :] = total

    def rz_copy(k):
        return send(
            zsend.at[lax.rem(z + k, Z)], zrecv.at[k - 1],
            rz_s.at[k - 1], rz_r.at[k - 1], *along_z(k),
        )

    def rz_start(n, carry):
        rz_copy(far_first(n)).start()
        return carry

    lax.fori_loop(0, Z - 1, rz_start, 0)
    settle()
    last = zsend[pl.ds(z, 1)][0]
    for k in range(1, Z):
        rz_copy(k).wait_recv()
        last = last + zrecv[k - 1]
    wg[...] = last

    def rz_sent(k, carry):
        rz_copy(k).wait_send()
        return carry

    lax.fori_loop(1, Z, rz_sent, 0)


def shards(inputs, queries, values, w_key, state_in, norm_in, out_gain, out_grad):
    docs, tokens, model = inputs.shape
    depth = w_key.shape[0]
    part = WIDTH // GROUP
    padded = part + 8
    rows_out = Z * Y_LO
    dma = pltpu.SemaphoreType.DMA
    vmem = pltpu.VMEM
    scan_buffers = [
        vmem((GROUP, padded, HEAD), BF16),
        vmem((GROUP, padded, HEAD), BF16),
        vmem((padded, HEAD), BF16),
        vmem((padded, HEAD), BF16),
        vmem((GROUP, padded, HEAD), BF16),
        vmem((GROUP, padded, HEAD), BF16),
    ]
    scan_sems = [dma((GROUP - 1,))] * 2 + [dma((1,))] * 2 + [dma((GROUP - 1,))] * 2
    scratch = (
        [
            vmem((tokens, model), BF16),
            vmem((tokens, WIDTH), BF16),
            vmem((tokens, WIDTH), BF16),
            vmem((HEADS, HEAD, HEAD), F32),
            vmem((HEADS, HEAD), F32),
            vmem((1, WIDTH), F32),
            vmem((tokens, WIDTH), BF16),
            vmem((Z, Y_LO, depth, WIDTH), BF16),
            vmem((Y_HI, X, CORES, rows_out, tokens), BF16),
            vmem((tokens, WIDTH), BF16),
            vmem((tokens, WIDTH), F32),
            vmem((tokens, WIDTH), BF16),
            vmem((tokens, WIDTH), F32),
            vmem((HEADS, tokens, tokens), BF16),
            vmem((tokens, WIDTH), F32),
            vmem((tokens, WIDTH), F32),
            vmem((tokens, WIDTH), F32),
            vmem((tokens, WIDTH), F32),
            vmem((tokens, WIDTH), BF16),
            vmem((tokens, WIDTH), F32),
            vmem((HEADS, HEAD, HEAD), BF16),
            vmem((tokens, WIDTH), F32),
            vmem((tokens, WIDTH), F32),
            vmem((tokens, WIDTH), BF16),
            vmem((HEADS, 1, HEAD), F32),
        ]
        + scan_buffers
        + scan_buffers
        + [
            vmem((Y_HI * rows_out, WIDTH), F32),
            vmem((X, Y_HI * rows_out, WIDTH), BF16),
            vmem((X, Y_HI * rows_out, WIDTH), BF16),
            vmem((2, rows_out, WIDTH), BF16),
            vmem((2, rows_out, WIDTH), BF16),
            vmem((2, Y_HI * rows_out, WIDTH), BF16),
            vmem((2, Y_HI * rows_out, WIDTH), BF16),
            vmem((RING_Y, Z, WIDTH), F32),
            vmem((RING_Y, Z, WIDTH), BF16),
            vmem((RING_Y - 1, Z, WIDTH), BF16),
            vmem((Z, 1, WIDTH), F32),
            vmem((Z - 1, 1, WIDTH), F32),
        ]
        + [dma((1,)), dma((7,))]
        + [dma((Z - 1,))] * 2
        + [dma((2 * Y_LO,))] * 2
        + [dma((Y_LO * 2,))] * 2
        + [dma((Y_LO + 1,))] * 2
        + scan_sems
        + scan_sems
        + [dma((X,))] * 2
        + [dma((2,))] * 4
        + [dma((RING_Y - 1,))] * 2
        + [dma((Z - 1,))] * 2
    )
    space = pl.BlockSpec(memory_space=pltpu.VMEM)
    anywhere = pl.BlockSpec(memory_space=pl.ANY)
    results = (
        ((3, tokens, WIDTH), BF16),
        ((tokens, model), BF16),
        ((1, WIDTH), F32),
    )
    outs = pl.pallas_call(
        body,
        out_shape=tuple(pltpu.VMEM(*r) for r in results),
        in_specs=[anywhere] * 8,
        out_specs=(space,) * 3,
        scratch_shapes=scratch,
        compiler_params=pltpu.CompilerParams(
            collective_id=0, has_side_effects=True, vmem_limit_bytes=56 * 1024 * 1024
        ),
    )(
        inputs[0],
        queries[0],
        values[0],
        w_key,
        state_in[0],
        norm_in[0],
        out_gain[None],
        out_grad[0],
    )
    big, inputs_grad, key_grad = outs
    return (big[0:1], inputs_grad[None], big[1:2], big[2:3], key_grad)


def solution(mesh):
    return jax.shard_map(
        shards,
        mesh=mesh,
        in_specs=(
            P("zero", "seq", None),
            P("zero", "seq", None),
            P("zero", "seq", None),
            P("zero", None),
            P("zero", None, None, None),
            P("zero", None, None),
            P(),
            P("zero", "seq", None),
        ),
        out_specs=(
            P("zero", "seq", None),
            P("zero", "seq", None),
            P("zero", "seq", None),
            P("zero", "seq", None),
            P(("seq", "zero"), None),
        ),
        check_vma=False,
    )
```
